512 devices in a mesh: dp: 4 (over x), context: 16 (over z_lo, core), head: 8 (over y, z_hi).
Axes of the slice: x: 4, y: 4, z: 16 (z_hi: 2, z_lo: 8; z = z_hi * 8 + z_lo), core: 2. Of those that a mesh axis runs over, the one named last changes fastest.
Arguments:
- hidden: bfloat16 [4, 3072, 4096], P('dp', 'context'), may hold values from -6 to 6
- queries: bfloat16 [4, 3072, 4096], P('dp', 'context', 'head'), may hold values from -216 to 216
- grad_out: bfloat16 [4, 3072, 4096], P('dp', 'context', 'head'), may hold values from -6 to 6
- segment: int32 [4, 3072], P('dp', 'context'), may hold values from 0 to 3, never falling along the last dimension, each value on 1 to 1920 neighbouring positions
- key_proj: bfloat16 [4096, 1024], P(('dp', 'context'), 'head'), may hold values from -0.09375 to 0.09375
- value_proj: bfloat16 [4096, 1024], P(('dp', 'context'), 'head'), may hold values from -0.09375 to 0.09375
Outputs:
- grad_queries: bfloat16 [4, 3072, 4096], P('dp', 'context', 'head')
- grad_key_proj: float32 [4096, 1024], P(('dp', 'context'), 'head')
- grad_value_proj: float32 [4096, 1024], P(('dp', 'context'), 'head')
The draws below stay inside these ranges and needn't reach their ends.
Inputs may be any that keep to these rules, and one draw needn't show every extreme that they name: segment ids never fall along a trace; each trace has 4 segments, one of exactly 1920 tokens.
All inputs are finite; a program needn't handle non-finite values.
Results may differ from the reference program's by a relative error of at most 0.04.
The reference program's roundings to bfloat16 on the way count: a program that leaves them out, or rounds other values in their place, can miss the bound.
Values may be sent and summed in bfloat16 or wider, within the bound.
A program may use at most 64 MiB of HBM per device.

```python
import math
import jax
import jax.numpy as jnp
import numpy as np
from jax import lax

D = 4096
HEADS = 32
KV_HEADS = 8
HEAD_DIM = 128
SEGS = 4
LEN = 3072
SEQS = 4
SEG_MOST = 1920


def draw_queries(key, part):
    base = jax.random.normal(key, (SEQS, LEN, HEADS * HEAD_DIM), jnp.float32)
    base = jnp.clip(base, -6.0, 6.0)
    return base.astype(jnp.bfloat16)


def strengthened(array, stream_key, source, target, blocks, factor):
    def block_of(axis_at):
        return (jnp.arange(array.shape[axis_at]) // (array.shape[axis_at] // blocks)).reshape((-1,) + (1,) * (array.ndim - 1 - axis_at))

    first = jax.random.permutation(stream_key, blocks)[block_of(target)]
    other_side = (block_of(target) + blocks // 2) % blocks
    return jnp.where((block_of(source) == first) | (block_of(source) == other_side), factor * array, array)


def levels(rng, extent, cuts, smallest, largest):
    def one(dim, blocks):
        draws = jax.random.uniform(jax.random.fold_in(jax.random.fold_in(rng, 6), dim), (blocks,), jnp.float32, smallest / len(cuts), largest / len(cuts))
        return jnp.repeat(jnp.exp(draws), extent[dim] // blocks).reshape((-1,) + (1,) * (len(extent) - dim - 1))

    loudness = one(*cuts[0])
    for cut in cuts[1:]:
        loudness = loudness * one(*cut)
    return loudness


def split_up(amount, total, most, slope):
    portions = [(1 << 20) // math.isqrt(rank ** slope) + 1 for rank in range(2, amount + 1)]
    spare, counts = total - most - (amount - 1), [1] * (amount - 1)
    while spare > 0:
        free = [i for i in range(amount - 1) if counts[i] < most]
        whole, remaining = sum([portions[i] for i in free]), spare
        for i in free:
            more = min(most - counts[i], max(1, remaining * portions[i] // whole), spare)
            counts[i] = counts[i] + more
            spare = spare - more
    return np.array([most] + counts)


def uneven(key, count, total, bound, slope):
    if count == 2:
        one = jax.random.randint(key, (), max(1, total - bound), min(bound, total - 1) + 1)
        return jnp.stack([one, total - one])
    lengths = jnp.asarray(split_up(count, total, bound, slope), jnp.int32)
    couples = (count - 1) // 2
    donor, sink = lengths[1:1 + 2 * couples:2], lengths[2:2 + 2 * couples:2]
    room = jnp.minimum(donor - 1, bound - sink)
    moved = jax.random.randint(jax.random.fold_in(key, 1), (couples,), 0, 1 << 20) % (room + 1)
    lengths = lengths.at[1:1 + 2 * couples:2].set(donor - moved).at[2:2 + 2 * couples:2].set(sink + moved)
    return lengths[jax.random.permutation(jax.random.fold_in(key, 2), count)]


def gaussian(key, extent, scale, most, shards=(), kind=jnp.bfloat16):
    gain = levels(key, extent, shards, -0.22, 0.18) if shards else 1.0
    values = jax.random.normal(key, extent, jnp.float32) * scale * gain
    return jnp.minimum(jnp.maximum(values, -most), most).astype(kind)


def bell_draw_with(key, dims, scale, bound, cuts, heavy, dtype=jnp.bfloat16):
    result = scale * jax.random.normal(key, dims, jnp.float32)
    if cuts:
        result = result * levels(key, dims, cuts, -0.22, 0.18)
    return jnp.clip(strengthened(result, jax.random.fold_in(key, 3), *heavy), -bound, bound).astype(dtype)


def setup_inputs(seed: int = 0) -> dict:
    key_of = jax.random.split(jax.random.key(seed), 7)
    hidden = bell_draw_with(key_of[0], (SEQS, LEN, D), 1.0, 6.0, ((0, 4), (1, 16)), (1, 2, 16, 2.0))
    queries = draw_queries(jax.random.fold_in(key_of[6], 71), 0)
    grad_out = gaussian(key_of[2], (SEQS, LEN, HEADS * HEAD_DIM), 1.0, 6.0, ((0, 4), (1, 16), (2, 8)))
    segment = jax.vmap(lambda own: jnp.searchsorted(jnp.cumsum(uneven(own, SEGS, LEN, SEG_MOST, 0)), jnp.arange(LEN), side="right"))(jax.random.split(key_of[3], SEQS)).reshape((SEQS, LEN)).astype(jnp.int32)
    key_proj = gaussian(key_of[4], (D, KV_HEADS * HEAD_DIM), D ** -0.5, 0.09375, ((0, 64), (1, 8)))
    value_proj = gaussian(key_of[5], (D, KV_HEADS * HEAD_DIM), D ** -0.5, 0.09375, ((0, 64), (1, 8)))
    return dict(hidden=hidden, queries=queries, grad_out=grad_out, segment=segment, key_proj=key_proj, value_proj=value_proj)


def group_grads(query_g, key_g, value_g, cot_g, same, scale):
    query_f = query_g.astype(jnp.float32)
    key_f = key_g.astype(jnp.float32)
    value_f = value_g.astype(jnp.float32)
    cot_f = cot_g.astype(jnp.float32)
    raw = jnp.einsum('gqd,kd->gqk', query_f, key_f) * scale
    raw = jnp.where(same[None], raw, -jnp.inf)
    top = jnp.max(raw, axis=-1, keepdims=True)
    total = jnp.sum(jnp.exp(raw - top), axis=-1, keepdims=True)
    log_total = top + jnp.log(total)
    probs = jnp.exp(raw - log_total)
    probs_b = lax.optimization_barrier(probs.astype(jnp.bfloat16)).astype(jnp.float32)
    output = jnp.einsum('gqk,kd->gqd', probs_b, value_f)
    output = lax.optimization_barrier(output.astype(jnp.bfloat16)).astype(jnp.float32)
    delta = jnp.sum(cot_f * output, axis=-1, keepdims=True)
    value_grad = jnp.einsum('gqk,gqd->kd', probs_b, cot_f)
    prob_grad = jnp.einsum('gqd,kd->gqk', cot_f, value_f)
    dscores = probs * (prob_grad - delta)
    dscores = lax.optimization_barrier(dscores.astype(jnp.bfloat16)).astype(jnp.float32)
    query_grad = (jnp.einsum('gqk,kd->gqd', dscores, key_f) * scale).astype(jnp.bfloat16)
    key_grad = jnp.einsum('gqk,gqd->kd', dscores, query_f) * scale
    return query_grad, key_grad, value_grad


def reference(hidden, queries, grad_out, segment, key_proj, value_proj):
    scale = HEAD_DIM ** -0.5
    group = HEADS // KV_HEADS
    grad_rows = []
    key_total = jnp.zeros((D, KV_HEADS * HEAD_DIM), jnp.float32)
    value_total = jnp.zeros((D, KV_HEADS * HEAD_DIM), jnp.float32)
    for trace in range(SEQS):
        rows_in = hidden[trace]
        keys = jnp.dot(rows_in, key_proj, preferred_element_type=jnp.float32).astype(jnp.bfloat16)
        values = jnp.dot(rows_in, value_proj, preferred_element_type=jnp.float32).astype(jnp.bfloat16)
        marks = segment[trace]
        same = marks[:, None] == marks[None, :]
        query_heads = queries[trace].reshape(LEN, KV_HEADS, group, HEAD_DIM).transpose(1, 2, 0, 3)
        cot_heads = grad_out[trace].reshape(LEN, KV_HEADS, group, HEAD_DIM).transpose(1, 2, 0, 3)
        key_heads = keys.reshape(LEN, KV_HEADS, HEAD_DIM).transpose(1, 0, 2)
        value_heads = values.reshape(LEN, KV_HEADS, HEAD_DIM).transpose(1, 0, 2)

        def one_group(parts):
            return group_grads(parts[0], parts[1], parts[2], parts[3], same, scale)

        query_grad, key_grad, value_grad = lax.map(one_group, (query_heads, key_heads, value_heads, cot_heads))
        grad_rows.append(query_grad.transpose(2, 0, 1, 3).reshape(LEN, HEADS * HEAD_DIM))
        key_flat = key_grad.transpose(1, 0, 2).reshape(LEN, KV_HEADS * HEAD_DIM).astype(jnp.bfloat16)
        value_flat = value_grad.transpose(1, 0, 2).reshape(LEN, KV_HEADS * HEAD_DIM).astype(jnp.bfloat16)
        key_total = key_total + jnp.dot(rows_in.T, key_flat, preferred_element_type=jnp.float32)
        value_total = value_total + jnp.dot(rows_in.T, value_flat, preferred_element_type=jnp.float32)
    return jnp.stack(grad_rows), key_total, value_total
```

```python
import jax
import jax.numpy as jnp
from jax import lax
from jax.sharding import PartitionSpec as P

HEADS = 32
KV_HEADS = 8
HEAD_DIM = 128


far_below = -1e30


def _bits(n):
    return n.bit_length() - 1


def _exchange(x, axis, size, bit):
    perm = [(i, i ^ (1 << bit)) for i in range(size)]
    return lax.ppermute(x, axis, perm)


def _my_bit(axis, bit):
    return ((lax.axis_index(axis) >> bit) & 1) == 1


def gather_blocks(x, steps, canon):
    cur = x
    dims = []
    for axis, size, bit in steps:
        recv = _exchange(cur, axis, size, bit)
        mine = _my_bit(axis, bit)
        cur = jnp.where(mine, jnp.stack([recv, cur]), jnp.stack([cur, recv]))
        dims.insert(0, (axis, bit))
    order = [dims.index(c) for c in canon]
    cur = jnp.transpose(cur, order + list(range(len(dims), cur.ndim)))
    return cur.reshape((-1,) + x.shape[1:])


def scatter_sum(x, steps, canon):
    nb = len(canon)
    block = x.shape[0] >> nb
    cur = x.reshape((2,) * nb + (block,) + x.shape[1:])
    dims = list(canon)
    for axis, size, bit in steps:
        at = dims.index((axis, bit))
        lo = lax.index_in_dim(cur, 0, at, keepdims=False)
        hi = lax.index_in_dim(cur, 1, at, keepdims=False)
        mine = _my_bit(axis, bit)
        keep = jnp.where(mine, hi, lo)
        send = jnp.where(mine, lo, hi)
        cur = keep + _exchange(send, axis, size, bit)
        dims.pop(at)
    return cur


def body(hidden, queries, grad_out, segment, key_proj, value_proj):
    tok_rows = hidden.shape[1]
    n_dp = lax.axis_size("dp")
    n_ctx = lax.axis_size("context")
    group = HEADS // KV_HEADS
    scale = HEAD_DIM ** (-0.5)
    width_kv = key_proj.shape[1]
    local_rows = hidden[0]

    ctx_canon = [("context", b) for b in reversed(range(_bits(n_ctx)))]
    dp_canon = [("dp", b) for b in reversed(range(_bits(n_dp)))]
    both_canon = dp_canon + ctx_canon

    def step(axis, bit):
        return (axis, n_dp if axis == "dp" else n_ctx, bit)

    far_first = [step(a, b) for a, b in both_canon[::-1]]
    far_first = sorted(far_first, key=lambda s: (-(s[2] + (1 if s[0] == "dp" else 0))))
    near_first = far_first[::-1]

    proj = jnp.concatenate([key_proj, value_proj], axis=1)
    proj_all = gather_blocks(proj, far_first, both_canon)
    kv = jnp.dot(local_rows, proj_all, preferred_element_type=jnp.float32).astype(jnp.bfloat16)
    marks_col = jnp.broadcast_to(segment[0].astype(jnp.bfloat16)[:, None], (tok_rows, 128))
    kvm = jnp.concatenate([kv, marks_col], axis=1)
    ctx_far_first = [step("context", b) for b in reversed(range(_bits(n_ctx)))]
    kvm_all = gather_blocks(kvm, ctx_far_first, ctx_canon)
    keys = kvm_all[:, :HEAD_DIM]
    values = kvm_all[:, HEAD_DIM:2 * HEAD_DIM]
    marks_all = kvm_all[:, 2 * HEAD_DIM]
    marks = segment[0].astype(jnp.bfloat16)

    q = queries[0].reshape(tok_rows, group, HEAD_DIM)
    do = grad_out[0].reshape(tok_rows, group, HEAD_DIM)
    same = (marks[:, None] == marks_all[None, :])[:, None, :]
    raw = jnp.einsum("qgd,kd->qgk", q, keys, preferred_element_type=jnp.float32) * scale
    raw = jnp.where(same, raw, far_below)
    top = jnp.max(raw, axis=-1)
    total = jnp.sum(jnp.where(same, jnp.exp(raw - top[..., None]), 0.0), axis=-1)
    log_total = top + jnp.log(total)
    probs = jnp.where(same, jnp.exp(raw - log_total[..., None]), 0.0)
    probs_b = probs.astype(jnp.bfloat16)
    output = jnp.einsum("qgk,kd->qgd", probs_b, values, preferred_element_type=jnp.float32).astype(
        jnp.bfloat16
    )
    delta = jnp.sum(do.astype(jnp.float32) * output.astype(jnp.float32), axis=-1)
    value_part = jnp.einsum("qgk,qgd->kd", probs_b, do, preferred_element_type=jnp.float32)
    prob_grad = jnp.einsum("qgd,kd->qgk", do, values, preferred_element_type=jnp.float32)
    dscores = (probs * (prob_grad - delta[..., None])).astype(jnp.bfloat16)
    grad_q = (
        jnp.einsum("qgk,kd->qgd", dscores, keys, preferred_element_type=jnp.float32) * scale
    ).astype(jnp.bfloat16)
    key_part = jnp.einsum("qgk,qgd->kd", dscores, q, preferred_element_type=jnp.float32) * scale

    kv_part = jnp.concatenate([key_part, value_part], axis=1)
    ctx_near_first = ctx_far_first[::-1]
    kv_grad = scatter_sum(kv_part, ctx_near_first, ctx_canon).astype(jnp.bfloat16)

    proj_part = jnp.einsum("td,tc->dc", local_rows, kv_grad, preferred_element_type=jnp.float32)
    summed = scatter_sum(proj_part, near_first, both_canon)
    grad_queries = grad_q.reshape(1, tok_rows, group * HEAD_DIM)
    return (grad_queries, summed[:, :width_kv], summed[:, width_kv:])


def solution(mesh):
    placed = (
        P("dp", "context", None),
        P("dp", "context", "head"),
        P("dp", "context", "head"),
        P("dp", "context"),
        P(("dp", "context"), "head"),
        P(("dp", "context"), "head"),
    )
    return jax.shard_map(
        body,
        mesh=mesh,
        in_specs=placed,
        out_specs=(
            P("dp", "context", "head"),
            P(("dp", "context"), "head"),
            P(("dp", "context"), "head"),
        ),
        check_vma=False,
    )
```

```python
import jax
import jax.numpy as jnp
from jax import lax
from jax.sharding import PartitionSpec as P

HEADS = 32
KV_HEADS = 8
HEAD_DIM = 128


far_below = -1e30


def _bits(n):
    return n.bit_length() - 1


def _exchange(x, axis, size, bit):
    perm = [(i, i ^ (1 << bit)) for i in range(size)]
    return lax.ppermute(x, axis, perm)


def _my_bit(axis, bit):
    return ((lax.axis_index(axis) >> bit) & 1) == 1


def gather_blocks(x, steps, canon):
    cur = x
    dims = []
    for axis, size, bit in steps:
        recv = _exchange(cur, axis, size, bit)
        mine = _my_bit(axis, bit)
        cur = jnp.where(mine, jnp.stack([recv, cur]), jnp.stack([cur, recv]))
        dims.insert(0, (axis, bit))
    order = [dims.index(c) for c in canon]
    cur = jnp.transpose(cur, order + list(range(len(dims), cur.ndim)))
    return cur.reshape((-1,) + x.shape[1:])


def scatter_sum(x, steps, canon, acc=None):
    nb = len(canon)
    acc = acc or x.dtype
    block = x.shape[0] >> nb
    cur = x.reshape((2,) * nb + (block,) + x.shape[1:])
    dims = list(canon)
    for axis, size, bit in steps:
        at = dims.index((axis, bit))
        lo = lax.index_in_dim(cur, 0, at, keepdims=False)
        hi = lax.index_in_dim(cur, 1, at, keepdims=False)
        mine = _my_bit(axis, bit)
        keep = jnp.where(mine, hi, lo)
        send = jnp.where(mine, lo, hi)
        total = keep.astype(acc) + _exchange(send, axis, size, bit).astype(acc)
        cur = total if len(dims) == 1 else total.astype(x.dtype)
        dims.pop(at)
    return cur


def body(hidden, queries, grad_out, segment, key_proj, value_proj):
    tok_rows = hidden.shape[1]
    n_dp = lax.axis_size("dp")
    n_ctx = lax.axis_size("context")
    group = HEADS // KV_HEADS
    scale = HEAD_DIM ** (-0.5)
    width_kv = key_proj.shape[1]
    local_rows = hidden[0]

    ctx_canon = [("context", b) for b in reversed(range(_bits(n_ctx)))]
    dp_canon = [("dp", b) for b in reversed(range(_bits(n_dp)))]
    both_canon = dp_canon + ctx_canon

    def step(axis, bit):
        return (axis, n_dp if axis == "dp" else n_ctx, bit)

    far_first = [step(a, b) for a, b in both_canon[::-1]]
    far_first = sorted(far_first, key=lambda s: (-(s[2] + (1 if s[0] == "dp" else 0))))
    near_first = far_first[::-1]

    proj = jnp.concatenate([key_proj, value_proj], axis=1)
    proj_all = gather_blocks(proj, far_first, both_canon)
    kv = jnp.dot(local_rows, proj_all, preferred_element_type=jnp.float32).astype(jnp.bfloat16)
    marks = segment[0].astype(jnp.bfloat16)
    marks_row = jnp.pad(marks, (0, 2 * HEAD_DIM - tok_rows))[None, :]
    kvm = jnp.concatenate([kv, marks_row], axis=0)[None]
    ctx_far_first = [step("context", b) for b in reversed(range(_bits(n_ctx)))]
    kvm_all = gather_blocks(kvm, ctx_far_first, ctx_canon)
    keys = kvm_all[:, :tok_rows, :HEAD_DIM].reshape(-1, HEAD_DIM)
    values = kvm_all[:, :tok_rows, HEAD_DIM:].reshape(-1, HEAD_DIM)
    marks_all = kvm_all[:, tok_rows, :tok_rows].reshape(-1)

    q = queries[0].reshape(tok_rows, group, HEAD_DIM)
    do = grad_out[0].reshape(tok_rows, group, HEAD_DIM)
    same = (marks[:, None] == marks_all[None, :])[:, None, :]
    raw = jnp.einsum("qgd,kd->qgk", q, keys, preferred_element_type=jnp.float32) * scale
    raw = jnp.where(same, raw, far_below)
    top = jnp.max(raw, axis=-1)
    total = jnp.sum(jnp.where(same, jnp.exp(raw - top[..., None]), 0.0), axis=-1)
    log_total = top + jnp.log(total)
    probs = jnp.where(same, jnp.exp(raw - log_total[..., None]), 0.0)
    probs_b = probs.astype(jnp.bfloat16)
    output = jnp.einsum("qgk,kd->qgd", probs_b, values, preferred_element_type=jnp.float32).astype(
        jnp.bfloat16
    )
    delta = jnp.sum(do.astype(jnp.float32) * output.astype(jnp.float32), axis=-1)
    value_part = jnp.einsum("qgk,qgd->kd", probs_b, do, preferred_element_type=jnp.float32)
    prob_grad = jnp.einsum("qgd,kd->qgk", do, values, preferred_element_type=jnp.float32)
    dscores = (probs * (prob_grad - delta[..., None])).astype(jnp.bfloat16)
    grad_q = (
        jnp.einsum("qgk,kd->qgd", dscores, keys, preferred_element_type=jnp.float32) * scale
    ).astype(jnp.bfloat16)
    key_part = jnp.einsum("qgk,qgd->kd", dscores, q, preferred_element_type=jnp.float32) * scale

    kv_part = jnp.concatenate([key_part, value_part], axis=1).astype(jnp.bfloat16)
    ctx_near_first = ctx_far_first[::-1]
    kv_grad = scatter_sum(kv_part, ctx_near_first, ctx_canon, jnp.float32).astype(jnp.bfloat16)

    proj_part = jnp.einsum("td,tc->dc", local_rows, kv_grad, preferred_element_type=jnp.float32)
    summed = scatter_sum(proj_part, near_first, both_canon)
    grad_queries = grad_q.reshape(1, tok_rows, group * HEAD_DIM)
    return (grad_queries, summed[:, :width_kv], summed[:, width_kv:])


def solution(mesh):
    placed = (
        P("dp", "context", None),
        P("dp", "context", "head"),
        P("dp", "context", "head"),
        P("dp", "context"),
        P(("dp", "context"), "head"),
        P(("dp", "context"), "head"),
    )
    return jax.shard_map(
        body,
        mesh=mesh,
        in_specs=placed,
        out_specs=(
            P("dp", "context", "head"),
            P(("dp", "context"), "head"),
            P(("dp", "context"), "head"),
        ),
        check_vma=False,
    )
```

```python
import jax
import jax.numpy as jnp
from jax import lax
from jax.sharding import PartitionSpec as P

HEADS = 32
KV_HEADS = 8
HEAD_DIM = 128


far_below = -1e30


def _bits(n):
    return n.bit_length() - 1


def _exchange(x, axis, size, bit):
    perm = [(i, i ^ (1 << bit)) for i in range(size)]
    return lax.ppermute(x, axis, perm)


def _my_bit(axis, bit):
    return ((lax.axis_index(axis) >> bit) & 1) == 1


def gather_blocks(x, steps, canon):
    cur = x
    dims = []
    for axis, size, bit in steps:
        recv = _exchange(cur, axis, size, bit)
        mine = _my_bit(axis, bit)
        cur = jnp.where(mine, jnp.stack([recv, cur]), jnp.stack([cur, recv]))
        dims.insert(0, (axis, bit))
    order = [dims.index(c) for c in canon]
    cur = jnp.transpose(cur, order + list(range(len(dims), cur.ndim)))
    return cur.reshape((-1,) + x.shape[1:])


def scatter_sum(x, steps, canon, acc=None):
    nb = len(canon)
    acc = acc or x.dtype
    block = x.shape[0] >> nb
    cur = x.reshape((2,) * nb + (block,) + x.shape[1:])
    dims = list(canon)
    for axis, size, bit in steps:
        at = dims.index((axis, bit))
        lo = lax.index_in_dim(cur, 0, at, keepdims=False)
        hi = lax.index_in_dim(cur, 1, at, keepdims=False)
        mine = _my_bit(axis, bit)
        keep = jnp.where(mine, hi, lo)
        send = jnp.where(mine, lo, hi)
        total = keep.astype(acc) + _exchange(send, axis, size, bit).astype(acc)
        cur = total if len(dims) == 1 else total.astype(x.dtype)
        dims.pop(at)
    return cur


def body(hidden, queries, grad_out, segment, key_proj, value_proj):
    tok_rows = hidden.shape[1]
    n_dp = lax.axis_size("dp")
    n_ctx = lax.axis_size("context")
    group = HEADS // KV_HEADS
    scale = HEAD_DIM ** (-0.5)
    width_kv = key_proj.shape[1]
    local_rows = hidden[0]

    ctx_canon = [("context", b) for b in reversed(range(_bits(n_ctx)))]
    dp_canon = [("dp", b) for b in reversed(range(_bits(n_dp)))]
    both_canon = dp_canon + ctx_canon

    def step(axis, bit):
        return (axis, n_dp if axis == "dp" else n_ctx, bit)

    ctx_far = [step("context", b) for b in reversed(range(_bits(n_ctx)))]
    dp_far = [step("dp", b) for b in reversed(range(_bits(n_dp)))]
    def interleave(first, second):
        out = []
        for k in range(max(len(first), len(second))):
            out += first[k:k + 1] + second[k:k + 1]
        return out

    order_a = ctx_far[:1] + interleave(ctx_far[1:-1], dp_far) + ctx_far[-1:]
    order_b = ctx_far[:1] + interleave(dp_far, ctx_far[1:-1]) + ctx_far[-1:]

    key_all = gather_blocks(key_proj, order_a, both_canon)
    value_all = gather_blocks(value_proj, order_b, both_canon)
    proj_all = jnp.concatenate([key_all, value_all], axis=1)
    kv = jnp.dot(local_rows, proj_all, preferred_element_type=jnp.float32).astype(jnp.bfloat16)
    marks = segment[0].astype(jnp.bfloat16)
    marks_row = jnp.pad(marks, (0, 2 * HEAD_DIM - tok_rows))[None, :]
    kvm = jnp.concatenate([kv, marks_row], axis=0)[None]
    ctx_far_first = ctx_far
    kvm_all = gather_blocks(kvm, ctx_far_first, ctx_canon)
    keys = kvm_all[:, :tok_rows, :HEAD_DIM].reshape(-1, HEAD_DIM)
    values = kvm_all[:, :tok_rows, HEAD_DIM:].reshape(-1, HEAD_DIM)
    marks_all = kvm_all[:, tok_rows, :tok_rows].reshape(-1)

    q = queries[0].reshape(tok_rows, group, HEAD_DIM)
    do = grad_out[0].reshape(tok_rows, group, HEAD_DIM)
    same = (marks[:, None] == marks_all[None, :])[:, None, :]
    raw = jnp.einsum("qgd,kd->qgk", q, keys, preferred_element_type=jnp.float32) * scale
    raw = jnp.where(same, raw, far_below)
    top = jnp.max(raw, axis=-1)
    total = jnp.sum(jnp.where(same, jnp.exp(raw - top[..., None]), 0.0), axis=-1)
    log_total = top + jnp.log(total)
    probs = jnp.where(same, jnp.exp(raw - log_total[..., None]), 0.0)
    probs_b = probs.astype(jnp.bfloat16)
    output = jnp.einsum("qgk,kd->qgd", probs_b, values, preferred_element_type=jnp.float32).astype(
        jnp.bfloat16
    )
    delta = jnp.sum(do.astype(jnp.float32) * output.astype(jnp.float32), axis=-1)
    value_part = jnp.einsum("qgk,qgd->kd", probs_b, do, preferred_element_type=jnp.float32)
    prob_grad = jnp.einsum("qgd,kd->qgk", do, values, preferred_element_type=jnp.float32)
    dscores = (probs * (prob_grad - delta[..., None])).astype(jnp.bfloat16)
    grad_q = (
        jnp.einsum("qgk,kd->qgd", dscores, keys, preferred_element_type=jnp.float32) * scale
    ).astype(jnp.bfloat16)
    key_part = jnp.einsum("qgk,qgd->kd", dscores, q, preferred_element_type=jnp.float32) * scale

    kv_part = jnp.concatenate([key_part, value_part], axis=1).astype(jnp.bfloat16)
    ctx_near_first = ctx_far_first[::-1]
    kv_grad = scatter_sum(kv_part, ctx_near_first, ctx_canon, jnp.float32).astype(jnp.bfloat16)

    proj_part = jnp.einsum("td,tc->dc", local_rows, kv_grad, preferred_element_type=jnp.float32)
    key_sum = scatter_sum(proj_part[:, :width_kv], order_a[::-1], both_canon)
    value_sum = scatter_sum(proj_part[:, width_kv:], order_b[::-1], both_canon)
    grad_queries = grad_q.reshape(1, tok_rows, group * HEAD_DIM)
    return (grad_queries, key_sum, value_sum)


def solution(mesh):
    placed = (
        P("dp", "context", None),
        P("dp", "context", "head"),
        P("dp", "context", "head"),
        P("dp", "context"),
        P(("dp", "context"), "head"),
        P(("dp", "context"), "head"),
    )
    return jax.shard_map(
        body,
        mesh=mesh,
        in_specs=placed,
        out_specs=(
            P("dp", "context", "head"),
            P(("dp", "context"), "head"),
            P(("dp", "context"), "head"),
        ),
        check_vma=False,
    )
```

```python
import jax
import jax.numpy as jnp
from jax import lax
from jax.experimental import pallas as pl
from jax.experimental.pallas import tpu as pltpu
from jax.sharding import PartitionSpec as P

HEADS = 32
KV_HEADS = 8
HEAD_DIM = 128


far_below = -1e30


def _bits(n):
    return n.bit_length() - 1


def _exchange(x, axis, size, bit):
    perm = [(i, i ^ (1 << bit)) for i in range(size)]
    return lax.ppermute(x, axis, perm)


def _my_bit(axis, bit):
    return ((lax.axis_index(axis) >> bit) & 1) == 1


def gather_blocks(x, steps, canon):
    cur = x
    dims = []
    for axis, size, bit in steps:
        recv = _exchange(cur, axis, size, bit)
        mine = _my_bit(axis, bit)
        cur = jnp.where(mine, jnp.stack([recv, cur]), jnp.stack([cur, recv]))
        dims.insert(0, (axis, bit))
    order = [dims.index(c) for c in canon]
    cur = jnp.transpose(cur, order + list(range(len(dims), cur.ndim)))
    return cur.reshape((-1,) + x.shape[1:])


def scatter_sum(x, steps, canon, acc=None):
    nb = len(canon)
    acc = acc or x.dtype
    block = x.shape[0] >> nb
    cur = x.reshape((2,) * nb + (block,) + x.shape[1:])
    dims = list(canon)
    for axis, size, bit in steps:
        at = dims.index((axis, bit))
        lo = lax.index_in_dim(cur, 0, at, keepdims=False)
        hi = lax.index_in_dim(cur, 1, at, keepdims=False)
        mine = _my_bit(axis, bit)
        keep = jnp.where(mine, hi, lo)
        send = jnp.where(mine, lo, hi)
        total = keep.astype(acc) + _exchange(send, axis, size, bit).astype(acc)
        cur = total if len(dims) == 1 else total.astype(x.dtype)
        dims.pop(at)
    return cur


def _attention_kernel(q_ref, do_ref, k_ref, v_ref, mq_ref, mk_ref, gq_ref, dkv_ref, dk_acc, dv_acc):
    scale = HEAD_DIM ** (-0.5)
    keys = k_ref[...]
    values = v_ref[...]
    same = mq_ref[...] == mk_ref[...]
    dk_acc[...] = jnp.zeros_like(dk_acc)
    dv_acc[...] = jnp.zeros_like(dv_acc)
    nt = (((1,), (1,)), ((), ()))
    for h in range(q_ref.shape[1] // HEAD_DIM):
        cols = slice(h * HEAD_DIM, (h + 1) * HEAD_DIM)
        qh = q_ref[:, cols]
        doh = do_ref[:, cols]
        raw = lax.dot_general(qh, keys, nt, preferred_element_type=jnp.float32) * scale
        raw = jnp.where(same, raw, far_below)
        top = jnp.max(raw, axis=1, keepdims=True)
        total = jnp.sum(jnp.exp(raw - top), axis=1, keepdims=True)
        probs = jnp.exp(raw - (top + jnp.log(total)))
        probs_b = probs.astype(jnp.bfloat16)
        out = jnp.dot(probs_b, values, preferred_element_type=jnp.float32).astype(jnp.bfloat16)
        delta = jnp.sum(doh.astype(jnp.float32) * out.astype(jnp.float32), axis=1, keepdims=True)
        dv_acc[...] += jnp.dot(probs.T.astype(jnp.bfloat16), doh, preferred_element_type=jnp.float32)
        prob_grad = lax.dot_general(doh, values, nt, preferred_element_type=jnp.float32)
        dscores = probs * (prob_grad - delta)
        gq_ref[:, cols] = (
            jnp.dot(dscores.astype(jnp.bfloat16), keys, preferred_element_type=jnp.float32) * scale
        ).astype(gq_ref.dtype)
        dk_acc[...] += jnp.dot(
            dscores.T.astype(jnp.bfloat16), qh, preferred_element_type=jnp.float32
        ) * scale
    dkv_ref[:, :HEAD_DIM] = dk_acc[...].astype(dkv_ref.dtype)
    dkv_ref[:, HEAD_DIM:] = dv_acc[...].astype(dkv_ref.dtype)


def attention_block(q, do, keys, values, mq, mk):
    rows, width = q.shape
    n_keys = keys.shape[0]
    heads = width // HEAD_DIM
    flops = 2 * rows * n_keys * HEAD_DIM * heads * 6
    vmem = pltpu.VMEM
    return pl.pallas_call(
        _attention_kernel,
        out_shape=(
            jax.ShapeDtypeStruct((rows, width), jnp.bfloat16),
            jax.ShapeDtypeStruct((n_keys, 2 * HEAD_DIM), jnp.bfloat16),
        ),
        in_specs=[pl.BlockSpec(memory_space=vmem)] * 6,
        out_specs=(pl.BlockSpec(memory_space=vmem), pl.BlockSpec(memory_space=vmem)),
        scratch_shapes=[
            pltpu.VMEM((n_keys, HEAD_DIM), jnp.float32),
            pltpu.VMEM((n_keys, HEAD_DIM), jnp.float32),
        ],
        cost_estimate=pl.CostEstimate(
            flops=flops,
            transcendentals=2 * rows * n_keys * heads,
            bytes_accessed=4 * rows * width * 2 + 4 * n_keys * HEAD_DIM * 2,
        ),
    )(q, do, keys, values, mq, mk)


def body(hidden, queries, grad_out, segment, key_proj, value_proj):
    tok_rows = hidden.shape[1]
    n_dp = lax.axis_size("dp")
    n_ctx = lax.axis_size("context")
    group = HEADS // KV_HEADS
    scale = HEAD_DIM ** (-0.5)
    width_kv = key_proj.shape[1]
    local_rows = hidden[0]

    ctx_canon = [("context", b) for b in reversed(range(_bits(n_ctx)))]
    dp_canon = [("dp", b) for b in reversed(range(_bits(n_dp)))]
    both_canon = dp_canon + ctx_canon

    def step(axis, bit):
        return (axis, n_dp if axis == "dp" else n_ctx, bit)

    ctx_far = [step("context", b) for b in reversed(range(_bits(n_ctx)))]
    dp_far = [step("dp", b) for b in reversed(range(_bits(n_dp)))]
    def interleave(first, second):
        out = []
        for k in range(max(len(first), len(second))):
            out += first[k:k + 1] + second[k:k + 1]
        return out

    order_a = ctx_far[:1] + interleave(ctx_far[1:-1], dp_far) + ctx_far[-1:]
    order_b = ctx_far[:1] + interleave(dp_far, ctx_far[1:-1]) + ctx_far[-1:]

    key_all = gather_blocks(key_proj, order_a, both_canon)
    value_all = gather_blocks(value_proj, order_b, both_canon)
    proj_all = jnp.concatenate([key_all, value_all], axis=1)
    kv = jnp.dot(local_rows, proj_all, preferred_element_type=jnp.float32).astype(jnp.bfloat16)
    marks = segment[0].astype(jnp.bfloat16)
    marks_row = jnp.pad(marks, (0, 2 * HEAD_DIM - tok_rows))[None, :]
    kvm = jnp.concatenate([kv, marks_row], axis=0)[None]
    ctx_far_first = ctx_far
    kvm_all = gather_blocks(kvm, ctx_far_first, ctx_canon)
    keys = kvm_all[:, :tok_rows, :HEAD_DIM].reshape(-1, HEAD_DIM)
    values = kvm_all[:, :tok_rows, HEAD_DIM:].reshape(-1, HEAD_DIM)
    marks_all = kvm_all[:, tok_rows, :tok_rows].reshape(-1)

    mq = marks.astype(jnp.float32)[:, None]
    mk = marks_all.astype(jnp.float32)[None, :]
    grad_q, kv_part = attention_block(queries[0], grad_out[0], keys, values, mq, mk)
    ctx_near_first = ctx_far_first[::-1]
    kv_grad = scatter_sum(kv_part, ctx_near_first, ctx_canon, jnp.float32).astype(jnp.bfloat16)

    proj_part = jnp.einsum("td,tc->dc", local_rows, kv_grad, preferred_element_type=jnp.float32)
    key_sum = scatter_sum(proj_part[:, :width_kv], order_a[::-1], both_canon)
    value_sum = scatter_sum(proj_part[:, width_kv:], order_b[::-1], both_canon)
    grad_queries = grad_q[None]
    return (grad_queries, key_sum, value_sum)


def solution(mesh):
    placed = (
        P("dp", "context", None),
        P("dp", "context", "head"),
        P("dp", "context", "head"),
        P("dp", "context"),
        P(("dp", "context"), "head"),
        P(("dp", "context"), "head"),
    )
    return jax.shard_map(
        body,
        mesh=mesh,
        in_specs=placed,
        out_specs=(
            P("dp", "context", "head"),
            P(("dp", "context"), "head"),
            P(("dp", "context"), "head"),
        ),
        check_vma=False,
    )
```

```python
import jax
import jax.numpy as jnp
from jax import lax
from jax.experimental import pallas as pl
from jax.experimental.pallas import tpu as pltpu
from jax.sharding import PartitionSpec as P

HEADS = 32
KV_HEADS = 8
HEAD_DIM = 128


far_below = -1e30


def _bits(n):
    return n.bit_length() - 1


def _exchange(x, axis, size, bit):
    perm = [(i, i ^ (1 << bit)) for i in range(size)]
    return lax.ppermute(x, axis, perm)


def _my_bit(axis, bit):
    return ((lax.axis_index(axis) >> bit) & 1) == 1


def gather_blocks(x, steps, canon):
    cur = x
    dims = []
    for axis, size, bit in steps:
        recv = _exchange(cur, axis, size, bit)
        mine = _my_bit(axis, bit)
        cur = jnp.where(mine, jnp.stack([recv, cur]), jnp.stack([cur, recv]))
        dims.insert(0, (axis, bit))
    order = [dims.index(c) for c in canon]
    cur = jnp.transpose(cur, order + list(range(len(dims), cur.ndim)))
    return cur.reshape((-1,) + x.shape[1:])


def scatter_sum(x, steps, canon, acc=None):
    nb = len(canon)
    acc = acc or x.dtype
    block = x.shape[0] >> nb
    cur = x.reshape((2,) * nb + (block,) + x.shape[1:])
    dims = list(canon)
    for axis, size, bit in steps:
        at = dims.index((axis, bit))
        lo = lax.index_in_dim(cur, 0, at, keepdims=False)
        hi = lax.index_in_dim(cur, 1, at, keepdims=False)
        mine = _my_bit(axis, bit)
        keep = jnp.where(mine, hi, lo)
        send = jnp.where(mine, lo, hi)
        total = keep.astype(acc) + _exchange(send, axis, size, bit).astype(acc)
        cur = total if len(dims) == 1 else total.astype(x.dtype)
        dims.pop(at)
    return cur


def gather_relative(x, steps):
    cur = x
    for axis, size, bit in steps:
        cur = jnp.stack([cur, _exchange(cur, axis, size, bit)])
    return cur


def scatter_relative(x, steps):
    dims = [bit for _, _, bit in steps][::-1]
    cur = x
    for axis, size, bit in steps[::-1]:
        at = dims.index(bit)
        keep = lax.index_in_dim(cur, 0, at, keepdims=False)
        send = lax.index_in_dim(cur, 1, at, keepdims=False)
        total = keep.astype(jnp.float32) + _exchange(send, axis, size, bit).astype(jnp.float32)
        cur = total if len(dims) == 1 else total.astype(x.dtype)
        dims.pop(at)
    return cur


def _attention_kernel(q_ref, do_ref, k_ref, v_ref, mq_ref, mk_ref, gq_ref, dkv_ref, dk_acc, dv_acc):
    scale = HEAD_DIM ** (-0.5)
    keys = k_ref[...]
    values = v_ref[...]
    same = mq_ref[...] == mk_ref[...]
    dk_acc[...] = jnp.zeros_like(dk_acc)
    dv_acc[...] = jnp.zeros_like(dv_acc)
    nt = (((1,), (1,)), ((), ()))
    for h in range(q_ref.shape[1] // HEAD_DIM):
        cols = slice(h * HEAD_DIM, (h + 1) * HEAD_DIM)
        qh = q_ref[:, cols]
        doh = do_ref[:, cols]
        raw = lax.dot_general(qh, keys, nt, preferred_element_type=jnp.float32) * scale
        raw = jnp.where(same, raw, far_below)
        top = jnp.max(raw, axis=1, keepdims=True)
        total = jnp.sum(jnp.exp(raw - top), axis=1, keepdims=True)
        probs = jnp.exp(raw - (top + jnp.log(total)))
        probs_b = probs.astype(jnp.bfloat16)
        out = jnp.dot(probs_b, values, preferred_element_type=jnp.float32).astype(jnp.bfloat16)
        delta = jnp.sum(doh.astype(jnp.float32) * out.astype(jnp.float32), axis=1, keepdims=True)
        dv_acc[...] += jnp.dot(probs.T.astype(jnp.bfloat16), doh, preferred_element_type=jnp.float32)
        prob_grad = lax.dot_general(doh, values, nt, preferred_element_type=jnp.float32)
        dscores = probs * (prob_grad - delta)
        gq_ref[:, cols] = (
            jnp.dot(dscores.astype(jnp.bfloat16), keys, preferred_element_type=jnp.float32) * scale
        ).astype(gq_ref.dtype)
        dk_acc[...] += jnp.dot(
            dscores.T.astype(jnp.bfloat16), qh, preferred_element_type=jnp.float32
        ) * scale
    dkv_ref[:, :HEAD_DIM] = dk_acc[...].astype(dkv_ref.dtype)
    dkv_ref[:, HEAD_DIM:] = dv_acc[...].astype(dkv_ref.dtype)


def attention_block(q, do, keys, values, mq, mk):
    rows, width = q.shape
    n_keys = keys.shape[0]
    heads = width // HEAD_DIM
    flops = 2 * rows * n_keys * HEAD_DIM * heads * 6
    vmem = pltpu.VMEM
    return pl.pallas_call(
        _attention_kernel,
        out_shape=(
            jax.ShapeDtypeStruct((rows, width), jnp.bfloat16),
            jax.ShapeDtypeStruct((n_keys, 2 * HEAD_DIM), jnp.bfloat16),
        ),
        in_specs=[pl.BlockSpec(memory_space=vmem)] * 6,
        out_specs=(pl.BlockSpec(memory_space=vmem), pl.BlockSpec(memory_space=vmem)),
        scratch_shapes=[
            pltpu.VMEM((n_keys, HEAD_DIM), jnp.float32),
            pltpu.VMEM((n_keys, HEAD_DIM), jnp.float32),
        ],
        cost_estimate=pl.CostEstimate(
            flops=flops,
            transcendentals=2 * rows * n_keys * heads,
            bytes_accessed=4 * rows * width * 2 + 4 * n_keys * HEAD_DIM * 2,
        ),
    )(q, do, keys, values, mq, mk)


def body(hidden, queries, grad_out, segment, key_proj, value_proj):
    tok_rows = hidden.shape[1]
    n_dp = lax.axis_size("dp")
    n_ctx = lax.axis_size("context")
    group = HEADS // KV_HEADS
    scale = HEAD_DIM ** (-0.5)
    width_kv = key_proj.shape[1]
    local_rows = hidden[0]

    ctx_canon = [("context", b) for b in reversed(range(_bits(n_ctx)))]
    dp_canon = [("dp", b) for b in reversed(range(_bits(n_dp)))]
    both_canon = dp_canon + ctx_canon

    def step(axis, bit):
        return (axis, n_dp if axis == "dp" else n_ctx, bit)

    ctx_far = [step("context", b) for b in reversed(range(_bits(n_ctx)))]
    dp_far = [step("dp", b) for b in reversed(range(_bits(n_dp)))]
    def interleave(first, second):
        out = []
        for k in range(max(len(first), len(second))):
            out += first[k:k + 1] + second[k:k + 1]
        return out

    order_a = ctx_far[:1] + interleave(ctx_far[1:-1], dp_far) + ctx_far[-1:]
    order_b = ctx_far[:1] + interleave(dp_far, ctx_far[1:-1]) + ctx_far[-1:]

    far_first = ctx_far[:1] + interleave(ctx_far[1:-1], dp_far) + ctx_far[-1:]
    proj = jnp.concatenate([key_proj, value_proj], axis=1)
    proj_all = gather_blocks(proj, far_first, both_canon)
    kv = jnp.dot(local_rows, proj_all, preferred_element_type=jnp.float32).astype(jnp.bfloat16)
    marks = segment[0].astype(jnp.bfloat16)
    marks_row = jnp.pad(marks, (0, 2 * HEAD_DIM - tok_rows))[None, :]
    kvm = jnp.concatenate([kv, marks_row], axis=0)[None]
    kvm_all = gather_relative(kvm, ctx_far).reshape((-1,) + kvm.shape[1:])
    keys = kvm_all[:, :tok_rows, :HEAD_DIM].reshape(-1, HEAD_DIM)
    values = kvm_all[:, :tok_rows, HEAD_DIM:].reshape(-1, HEAD_DIM)
    marks_all = kvm_all[:, tok_rows, :tok_rows].reshape(-1)

    mq = marks.astype(jnp.float32)[:, None]
    mk = marks_all.astype(jnp.float32)[None, :]
    grad_q, kv_part = attention_block(queries[0], grad_out[0], keys, values, mq, mk)
    kv_blocks = kv_part.reshape((2,) * len(ctx_far) + (tok_rows, kv_part.shape[1]))
    kv_grad = scatter_relative(kv_blocks, ctx_far).astype(jnp.bfloat16)

    proj_part = jnp.einsum("td,tc->dc", local_rows, kv_grad, preferred_element_type=jnp.float32)
    key_sum = scatter_sum(proj_part[:, :width_kv], order_a[::-1], both_canon)
    value_sum = scatter_sum(proj_part[:, width_kv:], order_b[::-1], both_canon)
    grad_queries = grad_q[None]
    return (grad_queries, key_sum, value_sum)


def solution(mesh):
    placed = (
        P("dp", "context", None),
        P("dp", "context", "head"),
        P("dp", "context", "head"),
        P("dp", "context"),
        P(("dp", "context"), "head"),
        P(("dp", "context"), "head"),
    )
    return jax.shard_map(
        body,
        mesh=mesh,
        in_specs=placed,
        out_specs=(
            P("dp", "context", "head"),
            P(("dp", "context"), "head"),
            P(("dp", "context"), "head"),
        ),
        check_vma=False,
    )
```

```python
import jax
import jax.numpy as jnp
from jax import lax
from jax.experimental import pallas as pl
from jax.experimental.pallas import tpu as pltpu
from jax.sharding import PartitionSpec as P

HEADS = 32
KV_HEADS = 8
HEAD_DIM = 128


far_below = -1e30


def _bits(n):
    return n.bit_length() - 1


def _exchange(x, axis, size, bit):
    perm = [(i, i ^ (1 << bit)) for i in range(size)]
    return lax.ppermute(x, axis, perm)


def _my_bit(axis, bit):
    return ((lax.axis_index(axis) >> bit) & 1) == 1


def gather_blocks(x, steps, canon):
    cur = x
    dims = []
    for axis, size, bit in steps:
        recv = _exchange(cur, axis, size, bit)
        mine = _my_bit(axis, bit)
        cur = jnp.where(mine, jnp.stack([recv, cur]), jnp.stack([cur, recv]))
        dims.insert(0, (axis, bit))
    order = [dims.index(c) for c in canon]
    cur = jnp.transpose(cur, order + list(range(len(dims), cur.ndim)))
    return cur.reshape((-1,) + x.shape[1:])


def scatter_sum(x, steps, canon, acc=None):
    nb = len(canon)
    acc = acc or x.dtype
    block = x.shape[0] >> nb
    cur = x.reshape((2,) * nb + (block,) + x.shape[1:])
    dims = list(canon)
    for axis, size, bit in steps:
        at = dims.index((axis, bit))
        lo = lax.index_in_dim(cur, 0, at, keepdims=False)
        hi = lax.index_in_dim(cur, 1, at, keepdims=False)
        mine = _my_bit(axis, bit)
        keep = jnp.where(mine, hi, lo)
        send = jnp.where(mine, lo, hi)
        total = keep.astype(acc) + _exchange(send, axis, size, bit).astype(acc)
        cur = total if len(dims) == 1 else total.astype(x.dtype)
        dims.pop(at)
    return cur


def gather_relative(x, steps):
    cur = x
    for axis, size, bit in steps:
        cur = jnp.stack([cur, _exchange(cur, axis, size, bit)])
    return cur


def scatter_relative(x, steps):
    dims = [bit for _, _, bit in steps][::-1]
    cur = x
    for axis, size, bit in steps[::-1]:
        at = dims.index(bit)
        keep = lax.index_in_dim(cur, 0, at, keepdims=False)
        send = lax.index_in_dim(cur, 1, at, keepdims=False)
        total = keep.astype(jnp.float32) + _exchange(send, axis, size, bit).astype(jnp.float32)
        cur = total if len(dims) == 1 else total.astype(x.dtype)
        dims.pop(at)
    return cur


def _attention_kernel(q_ref, do_ref, k_ref, v_ref, mq_ref, mk_ref, gq_ref, dkv_ref, dk_acc, dv_acc):
    scale = HEAD_DIM ** (-0.5)
    keys = k_ref[...]
    values = v_ref[...]
    same = mq_ref[...] == mk_ref[...]
    dk_acc[...] = jnp.zeros_like(dk_acc)
    dv_acc[...] = jnp.zeros_like(dv_acc)
    nt = (((1,), (1,)), ((), ()))
    for h in range(q_ref.shape[1] // HEAD_DIM):
        cols = slice(h * HEAD_DIM, (h + 1) * HEAD_DIM)
        qh = q_ref[:, cols]
        doh = do_ref[:, cols]
        raw = lax.dot_general(qh, keys, nt, preferred_element_type=jnp.float32) * scale
        raw = jnp.where(same, raw, far_below)
        top = jnp.max(raw, axis=1, keepdims=True)
        total = jnp.sum(jnp.exp(raw - top), axis=1, keepdims=True)
        probs = jnp.exp(raw - (top + jnp.log(total)))
        probs_b = probs.astype(jnp.bfloat16)
        out = jnp.dot(probs_b, values, preferred_element_type=jnp.float32).astype(jnp.bfloat16)
        delta = jnp.sum(doh.astype(jnp.float32) * out.astype(jnp.float32), axis=1, keepdims=True)
        dv_acc[...] += jnp.dot(probs.T.astype(jnp.bfloat16), doh, preferred_element_type=jnp.float32)
        prob_grad = lax.dot_general(doh, values, nt, preferred_element_type=jnp.float32)
        dscores = probs * (prob_grad - delta)
        gq_ref[:, cols] = (
            jnp.dot(dscores.astype(jnp.bfloat16), keys, preferred_element_type=jnp.float32) * scale
        ).astype(gq_ref.dtype)
        dk_acc[...] += jnp.dot(
            dscores.T.astype(jnp.bfloat16), qh, preferred_element_type=jnp.float32
        ) * scale
    dkv_ref[:, :HEAD_DIM] = dk_acc[...].astype(dkv_ref.dtype)
    dkv_ref[:, HEAD_DIM:] = dv_acc[...].astype(dkv_ref.dtype)


def attention_block(q, do, keys, values, mq, mk):
    rows, width = q.shape
    n_keys = keys.shape[0]
    heads = width // HEAD_DIM
    flops = 2 * rows * n_keys * HEAD_DIM * heads * 6
    vmem = pltpu.VMEM
    return pl.pallas_call(
        _attention_kernel,
        out_shape=(
            jax.ShapeDtypeStruct((rows, width), jnp.bfloat16),
            jax.ShapeDtypeStruct((n_keys, 2 * HEAD_DIM), jnp.bfloat16),
        ),
        in_specs=[pl.BlockSpec(memory_space=vmem)] * 6,
        out_specs=(pl.BlockSpec(memory_space=vmem), pl.BlockSpec(memory_space=vmem)),
        scratch_shapes=[
            pltpu.VMEM((n_keys, HEAD_DIM), jnp.float32),
            pltpu.VMEM((n_keys, HEAD_DIM), jnp.float32),
        ],
        cost_estimate=pl.CostEstimate(
            flops=flops,
            transcendentals=2 * rows * n_keys * heads,
            bytes_accessed=4 * rows * width * 2 + 4 * n_keys * HEAD_DIM * 2,
        ),
    )(q, do, keys, values, mq, mk)


def body(hidden, queries, grad_out, segment, key_proj, value_proj):
    tok_rows = hidden.shape[1]
    n_dp = lax.axis_size("dp")
    n_ctx = lax.axis_size("context")
    group = HEADS // KV_HEADS
    scale = HEAD_DIM ** (-0.5)
    width_kv = key_proj.shape[1]
    local_rows = hidden[0]

    ctx_canon = [("context", b) for b in reversed(range(_bits(n_ctx)))]
    dp_canon = [("dp", b) for b in reversed(range(_bits(n_dp)))]
    both_canon = dp_canon + ctx_canon

    def step(axis, bit):
        return (axis, n_dp if axis == "dp" else n_ctx, bit)

    ctx_far = [step("context", b) for b in reversed(range(_bits(n_ctx)))]
    dp_far = [step("dp", b) for b in reversed(range(_bits(n_dp)))]
    def interleave(first, second):
        out = []
        for k in range(max(len(first), len(second))):
            out += first[k:k + 1] + second[k:k + 1]
        return out

    order_a = ctx_far[:1] + interleave(ctx_far[1:-1], dp_far) + ctx_far[-1:]
    order_b = ctx_far[:1] + interleave(dp_far, ctx_far[1:-1]) + ctx_far[-1:]

    far_first = ctx_far[:1] + interleave(ctx_far[1:-1], dp_far) + ctx_far[-1:]
    proj = jnp.concatenate([key_proj, value_proj], axis=1)
    proj_all = gather_blocks(proj, far_first, both_canon)
    kv = jnp.dot(local_rows, proj_all, preferred_element_type=jnp.float32).astype(jnp.bfloat16)
    marks = segment[0].astype(jnp.bfloat16)
    marks_row = jnp.pad(marks, (0, 2 * HEAD_DIM - tok_rows))[None, :]
    kvm = jnp.concatenate([kv, marks_row], axis=0)[None]
    kvm_all = gather_relative(kvm, ctx_far).reshape((-1,) + kvm.shape[1:])
    keys = kvm_all[:, :tok_rows, :HEAD_DIM].reshape(-1, HEAD_DIM)
    values = kvm_all[:, :tok_rows, HEAD_DIM:].reshape(-1, HEAD_DIM)
    marks_all = kvm_all[:, tok_rows, :tok_rows].reshape(-1)

    mq = marks.astype(jnp.float32)[:, None]
    mk = marks_all.astype(jnp.float32)[None, :]
    grad_q, kv_part = attention_block(queries[0], grad_out[0], keys, values, mq, mk)
    kv_blocks = kv_part.reshape((2,) * len(ctx_far) + (tok_rows, kv_part.shape[1]))
    kv_grad = scatter_relative(kv_blocks, ctx_far).astype(jnp.bfloat16)

    dims_t = (((0,), (0,)), ((), ()))
    key_part = lax.dot_general(local_rows, kv_grad[:, :width_kv], dims_t, preferred_element_type=jnp.float32)
    value_part = lax.dot_general(local_rows, kv_grad[:, width_kv:], dims_t, preferred_element_type=jnp.float32)
    key_sum = scatter_sum(key_part.astype(jnp.bfloat16), order_a[::-1], both_canon, jnp.float32)
    value_sum = scatter_sum(value_part.astype(jnp.bfloat16), order_b[::-1], both_canon, jnp.float32)
    grad_queries = grad_q[None]
    return (grad_queries, key_sum, value_sum)


def solution(mesh):
    placed = (
        P("dp", "context", None),
        P("dp", "context", "head"),
        P("dp", "context", "head"),
        P("dp", "context"),
        P(("dp", "context"), "head"),
        P(("dp", "context"), "head"),
    )
    return jax.shard_map(
        body,
        mesh=mesh,
        in_specs=placed,
        out_specs=(
            P("dp", "context", "head"),
            P(("dp", "context"), "head"),
            P(("dp", "context"), "head"),
        ),
        check_vma=False,
    )
```

```python
import functools

import jax
import jax.numpy as jnp
from jax import lax
from jax.experimental import pallas as pl
from jax.experimental.pallas import tpu as pltpu
from jax.sharding import PartitionSpec as P

HEADS = 32
KV_HEADS = 8
HEAD_DIM = 128


far_below = -1e30


def _bits(n):
    return n.bit_length() - 1


def _exchange(x, axis, size, bit):
    perm = [(i, i ^ (1 << bit)) for i in range(size)]
    return lax.ppermute(x, axis, perm)


def _my_bit(axis, bit):
    return ((lax.axis_index(axis) >> bit) & 1) == 1


def gather_blocks(x, steps, canon):
    cur = x
    dims = []
    for axis, size, bit in steps:
        recv = _exchange(cur, axis, size, bit)
        mine = _my_bit(axis, bit)
        cur = jnp.where(mine, jnp.stack([recv, cur]), jnp.stack([cur, recv]))
        dims.insert(0, (axis, bit))
    order = [dims.index(c) for c in canon]
    cur = jnp.transpose(cur, order + list(range(len(dims), cur.ndim)))
    return cur.reshape((-1,) + x.shape[1:])


def scatter_sum(x, steps, canon, acc=None):
    nb = len(canon)
    acc = acc or x.dtype
    block = x.shape[0] >> nb
    cur = x.reshape((2,) * nb + (block,) + x.shape[1:])
    dims = list(canon)
    for axis, size, bit in steps:
        at = dims.index((axis, bit))
        lo = lax.index_in_dim(cur, 0, at, keepdims=False)
        hi = lax.index_in_dim(cur, 1, at, keepdims=False)
        mine = _my_bit(axis, bit)
        keep = jnp.where(mine, hi, lo)
        send = jnp.where(mine, lo, hi)
        total = keep.astype(acc) + _exchange(send, axis, size, bit).astype(acc)
        cur = total if len(dims) == 1 else total.astype(x.dtype)
        dims.pop(at)
    return cur


def gather_relative(x, steps):
    cur = x
    for axis, size, bit in steps:
        cur = jnp.stack([cur, _exchange(cur, axis, size, bit)])
    return cur


def scatter_relative(x, steps):
    dims = [bit for _, _, bit in steps][::-1]
    cur = x
    for axis, size, bit in steps[::-1]:
        at = dims.index(bit)
        keep = lax.index_in_dim(cur, 0, at, keepdims=False)
        send = lax.index_in_dim(cur, 1, at, keepdims=False)
        total = keep.astype(jnp.float32) + _exchange(send, axis, size, bit).astype(jnp.float32)
        cur = total if len(dims) == 1 else total.astype(x.dtype)
        dims.pop(at)
    return cur


def _gather_kernel(bits, x_ref, o_ref, held, send_sems, recv_sems, local_sem):
    me = lax.axis_index("context")
    partners = [lax.bitwise_xor(me, 1 << b) for b in bits]
    barrier = pltpu.get_barrier_semaphore()
    for p in partners:
        pl.semaphore_signal(barrier, inc=1, device_id={"context": p},
                            device_id_type=pl.DeviceIdType.MESH)
    pl.semaphore_wait(barrier, len(partners))
    local = pltpu.make_async_copy(x_ref, held.at[0:1], local_sem)
    local.start()
    for k, p in enumerate(partners):
        n = 1 << k
        if k == 1:
            local.wait()
        copy = pltpu.make_async_remote_copy(
            src_ref=x_ref if k == 0 else held.at[0:n],
            dst_ref=held.at[n:2 * n],
            send_sem=send_sems.at[k],
            recv_sem=recv_sems.at[k],
            device_id={"context": p},
            device_id_type=pl.DeviceIdType.MESH,
        )
        copy.start()
        copy.wait()
    if len(partners) < 2:
        local.wait()
    out = pltpu.make_async_copy(held, o_ref, local_sem)
    out.start()
    out.wait()


def context_gather(x, bits):
    n = 1 << len(bits)
    shape = (n,) + x.shape[1:]
    return pl.pallas_call(
        functools.partial(_gather_kernel, bits),
        out_shape=jax.ShapeDtypeStruct(shape, x.dtype),
        in_specs=[pl.BlockSpec(memory_space=pltpu.VMEM)],
        out_specs=pl.BlockSpec(memory_space=pltpu.VMEM),
        scratch_shapes=[
            pltpu.VMEM(shape, x.dtype),
            pltpu.SemaphoreType.DMA((len(bits),)),
            pltpu.SemaphoreType.DMA((len(bits),)),
            pltpu.SemaphoreType.DMA,
        ],
        compiler_params=pltpu.CompilerParams(collective_id=0, has_side_effects=True),
    )(x)


def _attention_kernel(q_ref, do_ref, k_ref, v_ref, mq_ref, mk_ref, gq_ref, dkv_ref, dk_acc, dv_acc):
    scale = HEAD_DIM ** (-0.5)
    keys = k_ref[...]
    values = v_ref[...]
    same = mq_ref[...] == mk_ref[...]
    dk_acc[...] = jnp.zeros_like(dk_acc)
    dv_acc[...] = jnp.zeros_like(dv_acc)
    nt = (((1,), (1,)), ((), ()))
    for h in range(q_ref.shape[1] // HEAD_DIM):
        cols = slice(h * HEAD_DIM, (h + 1) * HEAD_DIM)
        qh = q_ref[:, cols]
        doh = do_ref[:, cols]
        raw = lax.dot_general(qh, keys, nt, preferred_element_type=jnp.float32) * scale
        raw = jnp.where(same, raw, far_below)
        top = jnp.max(raw, axis=1, keepdims=True)
        total = jnp.sum(jnp.exp(raw - top), axis=1, keepdims=True)
        probs = jnp.exp(raw - (top + jnp.log(total)))
        probs_b = probs.astype(jnp.bfloat16)
        out = jnp.dot(probs_b, values, preferred_element_type=jnp.float32).astype(jnp.bfloat16)
        delta = jnp.sum(doh.astype(jnp.float32) * out.astype(jnp.float32), axis=1, keepdims=True)
        dv_acc[...] += jnp.dot(probs.T.astype(jnp.bfloat16), doh, preferred_element_type=jnp.float32)
        prob_grad = lax.dot_general(doh, values, nt, preferred_element_type=jnp.float32)
        dscores = probs * (prob_grad - delta)
        gq_ref[:, cols] = (
            jnp.dot(dscores.astype(jnp.bfloat16), keys, preferred_element_type=jnp.float32) * scale
        ).astype(gq_ref.dtype)
        dk_acc[...] += jnp.dot(
            dscores.T.astype(jnp.bfloat16), qh, preferred_element_type=jnp.float32
        ) * scale
    dkv_ref[:, :HEAD_DIM] = dk_acc[...].astype(dkv_ref.dtype)
    dkv_ref[:, HEAD_DIM:] = dv_acc[...].astype(dkv_ref.dtype)


def attention_block(q, do, keys, values, mq, mk):
    rows, width = q.shape
    n_keys = keys.shape[0]
    heads = width // HEAD_DIM
    flops = 2 * rows * n_keys * HEAD_DIM * heads * 6
    vmem = pltpu.VMEM
    return pl.pallas_call(
        _attention_kernel,
        out_shape=(
            jax.ShapeDtypeStruct((rows, width), jnp.bfloat16),
            jax.ShapeDtypeStruct((n_keys, 2 * HEAD_DIM), jnp.bfloat16),
        ),
        in_specs=[pl.BlockSpec(memory_space=vmem)] * 6,
        out_specs=(pl.BlockSpec(memory_space=vmem), pl.BlockSpec(memory_space=vmem)),
        scratch_shapes=[
            pltpu.VMEM((n_keys, HEAD_DIM), jnp.float32),
            pltpu.VMEM((n_keys, HEAD_DIM), jnp.float32),
        ],
        cost_estimate=pl.CostEstimate(
            flops=flops,
            transcendentals=2 * rows * n_keys * heads,
            bytes_accessed=4 * rows * width * 2 + 4 * n_keys * HEAD_DIM * 2,
        ),
    )(q, do, keys, values, mq, mk)


def body(hidden, queries, grad_out, segment, key_proj, value_proj):
    tok_rows = hidden.shape[1]
    n_dp = lax.axis_size("dp")
    n_ctx = lax.axis_size("context")
    group = HEADS // KV_HEADS
    scale = HEAD_DIM ** (-0.5)
    width_kv = key_proj.shape[1]
    local_rows = hidden[0]

    ctx_canon = [("context", b) for b in reversed(range(_bits(n_ctx)))]
    dp_canon = [("dp", b) for b in reversed(range(_bits(n_dp)))]
    both_canon = dp_canon + ctx_canon

    def step(axis, bit):
        return (axis, n_dp if axis == "dp" else n_ctx, bit)

    ctx_far = [step("context", b) for b in reversed(range(_bits(n_ctx)))]
    dp_far = [step("dp", b) for b in reversed(range(_bits(n_dp)))]
    def interleave(first, second):
        out = []
        for k in range(max(len(first), len(second))):
            out += first[k:k + 1] + second[k:k + 1]
        return out

    order_a = ctx_far[:1] + interleave(ctx_far[1:-1], dp_far) + ctx_far[-1:]
    order_b = ctx_far[:1] + interleave(dp_far, ctx_far[1:-1]) + ctx_far[-1:]

    far_first = ctx_far[:1] + interleave(ctx_far[1:-1], dp_far) + ctx_far[-1:]
    proj = jnp.concatenate([key_proj, value_proj], axis=1)
    proj_all = gather_blocks(proj, far_first, both_canon)
    kv = jnp.dot(local_rows, proj_all, preferred_element_type=jnp.float32).astype(jnp.bfloat16)
    marks = segment[0].astype(jnp.bfloat16)
    marks_row = jnp.pad(marks, (0, 2 * HEAD_DIM - tok_rows))[None, :]
    kvm = jnp.concatenate([kv, marks_row], axis=0)[None]
    kvm_all = context_gather(kvm, [bit for _, _, bit in ctx_far])
    keys = kvm_all[:, :tok_rows, :HEAD_DIM].reshape(-1, HEAD_DIM)
    values = kvm_all[:, :tok_rows, HEAD_DIM:].reshape(-1, HEAD_DIM)
    marks_all = kvm_all[:, tok_rows, :tok_rows].reshape(-1)

    mq = marks.astype(jnp.float32)[:, None]
    mk = marks_all.astype(jnp.float32)[None, :]
    grad_q, kv_part = attention_block(queries[0], grad_out[0], keys, values, mq, mk)
    kv_blocks = kv_part.reshape((2,) * len(ctx_far) + (tok_rows, kv_part.shape[1]))
    kv_grad = scatter_relative(kv_blocks, ctx_far).astype(jnp.bfloat16)

    dims_t = (((0,), (0,)), ((), ()))
    key_part = lax.dot_general(local_rows, kv_grad[:, :width_kv], dims_t, preferred_element_type=jnp.float32)
    value_part = lax.dot_general(local_rows, kv_grad[:, width_kv:], dims_t, preferred_element_type=jnp.float32)
    key_sum = scatter_sum(key_part.astype(jnp.bfloat16), order_a[::-1], both_canon, jnp.float32)
    value_sum = scatter_sum(value_part.astype(jnp.bfloat16), order_b[::-1], both_canon, jnp.float32)
    grad_queries = grad_q[None]
    return (grad_queries, key_sum, value_sum)


def solution(mesh):
    placed = (
        P("dp", "context", None),
        P("dp", "context", "head"),
        P("dp", "context", "head"),
        P("dp", "context"),
        P(("dp", "context"), "head"),
        P(("dp", "context"), "head"),
    )
    return jax.shard_map(
        body,
        mesh=mesh,
        in_specs=placed,
        out_specs=(
            P("dp", "context", "head"),
            P(("dp", "context"), "head"),
            P(("dp", "context"), "head"),
        ),
        check_vma=False,
    )
```

```python
import functools

import jax
import jax.numpy as jnp
from jax import lax
from jax.experimental import pallas as pl
from jax.experimental.pallas import tpu as pltpu
from jax.sharding import PartitionSpec as P

HEADS = 32
KV_HEADS = 8
HEAD_DIM = 128


far_below = -1e30


def _bits(n):
    return n.bit_length() - 1


def _exchange(x, axis, size, bit):
    perm = [(i, i ^ (1 << bit)) for i in range(size)]
    return lax.ppermute(x, axis, perm)


def _my_bit(axis, bit):
    return ((lax.axis_index(axis) >> bit) & 1) == 1


def gather_blocks(x, steps, canon):
    cur = x
    dims = []
    for axis, size, bit in steps:
        recv = _exchange(cur, axis, size, bit)
        mine = _my_bit(axis, bit)
        cur = jnp.where(mine, jnp.stack([recv, cur]), jnp.stack([cur, recv]))
        dims.insert(0, (axis, bit))
    order = [dims.index(c) for c in canon]
    cur = jnp.transpose(cur, order + list(range(len(dims), cur.ndim)))
    return cur.reshape((-1,) + x.shape[1:])


def scatter_sum(x, steps, canon, acc=None):
    nb = len(canon)
    acc = acc or x.dtype
    block = x.shape[0] >> nb
    cur = x.reshape((2,) * nb + (block,) + x.shape[1:])
    dims = list(canon)
    for axis, size, bit in steps:
        at = dims.index((axis, bit))
        lo = lax.index_in_dim(cur, 0, at, keepdims=False)
        hi = lax.index_in_dim(cur, 1, at, keepdims=False)
        mine = _my_bit(axis, bit)
        keep = jnp.where(mine, hi, lo)
        send = jnp.where(mine, lo, hi)
        total = keep.astype(acc) + _exchange(send, axis, size, bit).astype(acc)
        cur = total if len(dims) == 1 else total.astype(x.dtype)
        dims.pop(at)
    return cur


def gather_relative(x, steps):
    cur = x
    for axis, size, bit in steps:
        cur = jnp.stack([cur, _exchange(cur, axis, size, bit)])
    return cur


def scatter_relative(x, steps):
    dims = [bit for _, _, bit in steps][::-1]
    cur = x
    for axis, size, bit in steps[::-1]:
        at = dims.index(bit)
        keep = lax.index_in_dim(cur, 0, at, keepdims=False)
        send = lax.index_in_dim(cur, 1, at, keepdims=False)
        total = keep.astype(jnp.float32) + _exchange(send, axis, size, bit).astype(jnp.float32)
        cur = total if len(dims) == 1 else total.astype(x.dtype)
        dims.pop(at)
    return cur


def _gather_kernel(bits, x_ref, o_ref, held, send_sems, recv_sems, local_sem):
    me = lax.axis_index("context")
    partners = [lax.bitwise_xor(me, 1 << b) for b in bits]
    mesh = pl.DeviceIdType.MESH
    barrier = pltpu.get_barrier_semaphore()
    for p in partners:
        pl.semaphore_signal(barrier, inc=1, device_id={"context": p}, device_id_type=mesh)
    pl.semaphore_wait(barrier, len(partners))
    local = pltpu.make_async_copy(x_ref, held.at[0:1], local_sem)
    local.start()
    sends = []

    def push(src, lo, hi, j):
        base = 1 << j
        copy = pltpu.make_async_remote_copy(
            src_ref=src,
            dst_ref=held.at[base + lo:base + hi],
            send_sem=send_sems.at[len(sends)],
            recv_sem=recv_sems.at[j],
            device_id={"context": partners[j]},
            device_id_type=mesh,
        )
        copy.start()
        sends.append(copy)

    for j in range(len(partners)):
        push(x_ref, 0, 1, j)
    for i in range(len(partners)):
        lo, hi = 1 << i, 2 << i
        arrived = pltpu.make_async_remote_copy(
            src_ref=held.at[lo:hi],
            dst_ref=held.at[lo:hi],
            send_sem=send_sems.at[0],
            recv_sem=recv_sems.at[i],
            device_id={"context": partners[i]},
            device_id_type=mesh,
        )
        arrived.wait_recv()
        for j in range(i + 1, len(partners)):
            push(held.at[lo:hi], lo, hi, j)
    for copy in sends:
        copy.wait_send()
    local.wait()
    out = pltpu.make_async_copy(held, o_ref, local_sem)
    out.start()
    out.wait()


def context_gather(x, bits):
    n = 1 << len(bits)
    shape = (n,) + x.shape[1:]
    return pl.pallas_call(
        functools.partial(_gather_kernel, bits),
        out_shape=jax.ShapeDtypeStruct(shape, x.dtype),
        in_specs=[pl.BlockSpec(memory_space=pltpu.VMEM)],
        out_specs=pl.BlockSpec(memory_space=pltpu.VMEM),
        scratch_shapes=[
            pltpu.VMEM(shape, x.dtype),
            pltpu.SemaphoreType.DMA((len(bits) * (len(bits) + 1) // 2,)),
            pltpu.SemaphoreType.DMA((len(bits),)),
            pltpu.SemaphoreType.DMA,
        ],
        compiler_params=pltpu.CompilerParams(collective_id=0, has_side_effects=True),
    )(x)


def _attention_kernel(q_ref, do_ref, k_ref, v_ref, mq_ref, mk_ref, gq_ref, dkv_ref, dk_acc, dv_acc):
    scale = HEAD_DIM ** (-0.5)
    keys = k_ref[...]
    values = v_ref[...]
    same = mq_ref[...] == mk_ref[...]
    dk_acc[...] = jnp.zeros_like(dk_acc)
    dv_acc[...] = jnp.zeros_like(dv_acc)
    nt = (((1,), (1,)), ((), ()))
    for h in range(q_ref.shape[1] // HEAD_DIM):
        cols = slice(h * HEAD_DIM, (h + 1) * HEAD_DIM)
        qh = q_ref[:, cols]
        doh = do_ref[:, cols]
        raw = lax.dot_general(qh, keys, nt, preferred_element_type=jnp.float32) * scale
        raw = jnp.where(same, raw, far_below)
        top = jnp.max(raw, axis=1, keepdims=True)
        total = jnp.sum(jnp.exp(raw - top), axis=1, keepdims=True)
        probs = jnp.exp(raw - (top + jnp.log(total)))
        probs_b = probs.astype(jnp.bfloat16)
        out = jnp.dot(probs_b, values, preferred_element_type=jnp.float32).astype(jnp.bfloat16)
        delta = jnp.sum(doh.astype(jnp.float32) * out.astype(jnp.float32), axis=1, keepdims=True)
        dv_acc[...] += jnp.dot(probs.T.astype(jnp.bfloat16), doh, preferred_element_type=jnp.float32)
        prob_grad = lax.dot_general(doh, values, nt, preferred_element_type=jnp.float32)
        dscores = probs * (prob_grad - delta)
        gq_ref[:, cols] = (
            jnp.dot(dscores.astype(jnp.bfloat16), keys, preferred_element_type=jnp.float32) * scale
        ).astype(gq_ref.dtype)
        dk_acc[...] += jnp.dot(
            dscores.T.astype(jnp.bfloat16), qh, preferred_element_type=jnp.float32
        ) * scale
    dkv_ref[:, :HEAD_DIM] = dk_acc[...].astype(dkv_ref.dtype)
    dkv_ref[:, HEAD_DIM:] = dv_acc[...].astype(dkv_ref.dtype)


def attention_block(q, do, keys, values, mq, mk):
    rows, width = q.shape
    n_keys = keys.shape[0]
    heads = width // HEAD_DIM
    flops = 2 * rows * n_keys * HEAD_DIM * heads * 6
    vmem = pltpu.VMEM
    return pl.pallas_call(
        _attention_kernel,
        out_shape=(
            jax.ShapeDtypeStruct((rows, width), jnp.bfloat16),
            jax.ShapeDtypeStruct((n_keys, 2 * HEAD_DIM), jnp.bfloat16),
        ),
        in_specs=[pl.BlockSpec(memory_space=vmem)] * 6,
        out_specs=(pl.BlockSpec(memory_space=vmem), pl.BlockSpec(memory_space=vmem)),
        scratch_shapes=[
            pltpu.VMEM((n_keys, HEAD_DIM), jnp.float32),
            pltpu.VMEM((n_keys, HEAD_DIM), jnp.float32),
        ],
        cost_estimate=pl.CostEstimate(
            flops=flops,
            transcendentals=2 * rows * n_keys * heads,
            bytes_accessed=4 * rows * width * 2 + 4 * n_keys * HEAD_DIM * 2,
        ),
    )(q, do, keys, values, mq, mk)


def body(hidden, queries, grad_out, segment, key_proj, value_proj):
    tok_rows = hidden.shape[1]
    n_dp = lax.axis_size("dp")
    n_ctx = lax.axis_size("context")
    group = HEADS // KV_HEADS
    scale = HEAD_DIM ** (-0.5)
    width_kv = key_proj.shape[1]
    local_rows = hidden[0]

    ctx_canon = [("context", b) for b in reversed(range(_bits(n_ctx)))]
    dp_canon = [("dp", b) for b in reversed(range(_bits(n_dp)))]
    both_canon = dp_canon + ctx_canon

    def step(axis, bit):
        return (axis, n_dp if axis == "dp" else n_ctx, bit)

    ctx_far = [step("context", b) for b in reversed(range(_bits(n_ctx)))]
    dp_far = [step("dp", b) for b in reversed(range(_bits(n_dp)))]
    def interleave(first, second):
        out = []
        for k in range(max(len(first), len(second))):
            out += first[k:k + 1] + second[k:k + 1]
        return out

    order_a = ctx_far[:1] + interleave(ctx_far[1:-1], dp_far) + ctx_far[-1:]
    order_b = ctx_far[:1] + interleave(dp_far, ctx_far[1:-1]) + ctx_far[-1:]

    far_first = ctx_far[:1] + interleave(ctx_far[1:-1], dp_far) + ctx_far[-1:]
    proj = jnp.concatenate([key_proj, value_proj], axis=1)
    proj_all = gather_blocks(proj, far_first, both_canon)
    kv = jnp.dot(local_rows, proj_all, preferred_element_type=jnp.float32).astype(jnp.bfloat16)
    marks = segment[0].astype(jnp.bfloat16)
    marks_row = jnp.pad(marks, (0, 2 * HEAD_DIM - tok_rows))[None, :]
    kvm = jnp.concatenate([kv, marks_row], axis=0)[None]
    kvm_all = context_gather(kvm, [bit for _, _, bit in ctx_far])
    keys = kvm_all[:, :tok_rows, :HEAD_DIM].reshape(-1, HEAD_DIM)
    values = kvm_all[:, :tok_rows, HEAD_DIM:].reshape(-1, HEAD_DIM)
    marks_all = kvm_all[:, tok_rows, :tok_rows].reshape(-1)

    mq = marks.astype(jnp.float32)[:, None]
    mk = marks_all.astype(jnp.float32)[None, :]
    grad_q, kv_part = attention_block(queries[0], grad_out[0], keys, values, mq, mk)
    kv_blocks = kv_part.reshape((2,) * len(ctx_far) + (tok_rows, kv_part.shape[1]))
    kv_grad = scatter_relative(kv_blocks, ctx_far).astype(jnp.bfloat16)

    dims_t = (((0,), (0,)), ((), ()))
    key_part = lax.dot_general(local_rows, kv_grad[:, :width_kv], dims_t, preferred_element_type=jnp.float32)
    value_part = lax.dot_general(local_rows, kv_grad[:, width_kv:], dims_t, preferred_element_type=jnp.float32)
    key_sum = scatter_sum(key_part.astype(jnp.bfloat16), order_a[::-1], both_canon, jnp.float32)
    value_sum = scatter_sum(value_part.astype(jnp.bfloat16), order_b[::-1], both_canon, jnp.float32)
    grad_queries = grad_q[None]
    return (grad_queries, key_sum, value_sum)


def solution(mesh):
    placed = (
        P("dp", "context", None),
        P("dp", "context", "head"),
        P("dp", "context", "head"),
        P("dp", "context"),
        P(("dp", "context"), "head"),
        P(("dp", "context"), "head"),
    )
    return jax.shard_map(
        body,
        mesh=mesh,
        in_specs=placed,
        out_specs=(
            P("dp", "context", "head"),
            P(("dp", "context"), "head"),
            P(("dp", "context"), "head"),
        ),
        check_vma=False,
    )
```

```python
import functools

import jax
import jax.numpy as jnp
from jax import lax
from jax.experimental import pallas as pl
from jax.experimental.pallas import tpu as pltpu
from jax.sharding import PartitionSpec as P

HEADS = 32
KV_HEADS = 8
HEAD_DIM = 128


far_below = -1e30


def _bits(n):
    return n.bit_length() - 1


def _exchange(x, axis, size, bit):
    perm = [(i, i ^ (1 << bit)) for i in range(size)]
    return lax.ppermute(x, axis, perm)


def _my_bit(axis, bit):
    return ((lax.axis_index(axis) >> bit) & 1) == 1


def gather_blocks(x, steps, canon):
    cur = x
    dims = []
    for axis, size, bit in steps:
        recv = _exchange(cur, axis, size, bit)
        mine = _my_bit(axis, bit)
        cur = jnp.where(mine, jnp.stack([recv, cur]), jnp.stack([cur, recv]))
        dims.insert(0, (axis, bit))
    order = [dims.index(c) for c in canon]
    cur = jnp.transpose(cur, order + list(range(len(dims), cur.ndim)))
    return cur.reshape((-1,) + x.shape[1:])


def scatter_sum(x, steps, canon, acc=None):
    nb = len(canon)
    acc = acc or x.dtype
    block = x.shape[0] >> nb
    cur = x.reshape((2,) * nb + (block,) + x.shape[1:])
    dims = list(canon)
    for axis, size, bit in steps:
        at = dims.index((axis, bit))
        lo = lax.index_in_dim(cur, 0, at, keepdims=False)
        hi = lax.index_in_dim(cur, 1, at, keepdims=False)
        mine = _my_bit(axis, bit)
        keep = jnp.where(mine, hi, lo)
        send = jnp.where(mine, lo, hi)
        total = keep.astype(acc) + _exchange(send, axis, size, bit).astype(acc)
        cur = total if len(dims) == 1 else total.astype(x.dtype)
        dims.pop(at)
    return cur


def gather_relative(x, steps):
    cur = x
    for axis, size, bit in steps:
        cur = jnp.stack([cur, _exchange(cur, axis, size, bit)])
    return cur


def scatter_relative(x, steps):
    dims = [bit for _, _, bit in steps][::-1]
    cur = x
    for axis, size, bit in steps[::-1]:
        at = dims.index(bit)
        keep = lax.index_in_dim(cur, 0, at, keepdims=False)
        send = lax.index_in_dim(cur, 1, at, keepdims=False)
        total = keep.astype(jnp.float32) + _exchange(send, axis, size, bit).astype(jnp.float32)
        cur = total if len(dims) == 1 else total.astype(x.dtype)
        dims.pop(at)
    return cur


def _gather_kernel(steps, canonical, x_ref, o_ref, held, send_sems, recv_sems, local_sem):
    mesh = pl.DeviceIdType.MESH
    partners = [{axis: lax.bitwise_xor(lax.axis_index(axis), 1 << bit)} for axis, _, bit in steps]
    barrier = pltpu.get_barrier_semaphore()
    for p in partners:
        pl.semaphore_signal(barrier, inc=1, device_id=p, device_id_type=mesh)
    pl.semaphore_wait(barrier, len(partners))
    local = pltpu.make_async_copy(x_ref, held.at[0:1], local_sem)
    local.start()
    sends = []

    def push(src, lo, hi, j):
        base = 1 << j
        copy = pltpu.make_async_remote_copy(
            src_ref=src,
            dst_ref=held.at[base + lo:base + hi],
            send_sem=send_sems.at[len(sends)],
            recv_sem=recv_sems.at[j],
            device_id=partners[j],
            device_id_type=mesh,
        )
        copy.start()
        sends.append(copy)

    for j in range(len(partners)):
        push(x_ref, 0, 1, j)
    for i in range(len(partners)):
        lo, hi = 1 << i, 2 << i
        arrived = pltpu.make_async_remote_copy(
            src_ref=held.at[lo:hi],
            dst_ref=held.at[lo:hi],
            send_sem=send_sems.at[0],
            recv_sem=recv_sems.at[i],
            device_id=partners[i],
            device_id_type=mesh,
        )
        arrived.wait_recv()
        for j in range(i + 1, len(partners)):
            push(held.at[lo:hi], lo, hi, j)
    for copy in sends:
        copy.wait_send()
    local.wait()
    if canonical is None:
        out = pltpu.make_async_copy(held, o_ref, local_sem)
        out.start()
        out.wait()
        return
    weights = []
    me = 0
    for axis, size, bit in steps:
        idx = lax.axis_index(axis)
        mine = (idx // (1 << bit)) % 2
        weights.append(canonical[(axis, bit)] * (1 - 2 * mine))
    for axis, stride in canonical["origin"]:
        me = me + lax.axis_index(axis) * stride
    for r in range(1 << len(steps)):
        at = me
        for k in range(len(steps)):
            if (r >> k) & 1:
                at = at + weights[k]
        pltpu.make_async_copy(held.at[r:r + 1], o_ref.at[pl.ds(at, 1)], local_sem).start()
    pltpu.make_async_copy(held, o_ref, local_sem).wait()


def pair_gather(x, steps, collective_id, canonical=None):
    n = 1 << len(steps)
    shape = (n,) + x.shape[1:]
    return pl.pallas_call(
        functools.partial(_gather_kernel, steps, canonical),
        out_shape=jax.ShapeDtypeStruct(shape, x.dtype),
        in_specs=[pl.BlockSpec(memory_space=pltpu.VMEM)],
        out_specs=pl.BlockSpec(memory_space=pltpu.VMEM),
        scratch_shapes=[
            pltpu.VMEM(shape, x.dtype),
            pltpu.SemaphoreType.DMA((len(steps) * (len(steps) + 1) // 2,)),
            pltpu.SemaphoreType.DMA((len(steps),)),
            pltpu.SemaphoreType.DMA,
        ],
        compiler_params=pltpu.CompilerParams(collective_id=collective_id, has_side_effects=True),
    )(x)


def _attention_kernel(q_ref, do_ref, k_ref, v_ref, mq_ref, mk_ref, gq_ref, dkv_ref, dk_acc, dv_acc):
    scale = HEAD_DIM ** (-0.5)
    keys = k_ref[...]
    values = v_ref[...]
    same = mq_ref[...] == mk_ref[...]
    dk_acc[...] = jnp.zeros_like(dk_acc)
    dv_acc[...] = jnp.zeros_like(dv_acc)
    nt = (((1,), (1,)), ((), ()))
    for h in range(q_ref.shape[1] // HEAD_DIM):
        cols = slice(h * HEAD_DIM, (h + 1) * HEAD_DIM)
        qh = q_ref[:, cols]
        doh = do_ref[:, cols]
        raw = lax.dot_general(qh, keys, nt, preferred_element_type=jnp.float32) * scale
        raw = jnp.where(same, raw, far_below)
        top = jnp.max(raw, axis=1, keepdims=True)
        total = jnp.sum(jnp.exp(raw - top), axis=1, keepdims=True)
        probs = jnp.exp(raw - (top + jnp.log(total)))
        probs_b = probs.astype(jnp.bfloat16)
        out = jnp.dot(probs_b, values, preferred_element_type=jnp.float32).astype(jnp.bfloat16)
        delta = jnp.sum(doh.astype(jnp.float32) * out.astype(jnp.float32), axis=1, keepdims=True)
        dv_acc[...] += jnp.dot(probs.T.astype(jnp.bfloat16), doh, preferred_element_type=jnp.float32)
        prob_grad = lax.dot_general(doh, values, nt, preferred_element_type=jnp.float32)
        dscores = probs * (prob_grad - delta)
        gq_ref[:, cols] = (
            jnp.dot(dscores.astype(jnp.bfloat16), keys, preferred_element_type=jnp.float32) * scale
        ).astype(gq_ref.dtype)
        dk_acc[...] += jnp.dot(
            dscores.T.astype(jnp.bfloat16), qh, preferred_element_type=jnp.float32
        ) * scale
    dkv_ref[:, :HEAD_DIM] = dk_acc[...].astype(dkv_ref.dtype)
    dkv_ref[:, HEAD_DIM:] = dv_acc[...].astype(dkv_ref.dtype)


def attention_block(q, do, keys, values, mq, mk):
    rows, width = q.shape
    n_keys = keys.shape[0]
    heads = width // HEAD_DIM
    flops = 2 * rows * n_keys * HEAD_DIM * heads * 6
    vmem = pltpu.VMEM
    return pl.pallas_call(
        _attention_kernel,
        out_shape=(
            jax.ShapeDtypeStruct((rows, width), jnp.bfloat16),
            jax.ShapeDtypeStruct((n_keys, 2 * HEAD_DIM), jnp.bfloat16),
        ),
        in_specs=[pl.BlockSpec(memory_space=vmem)] * 6,
        out_specs=(pl.BlockSpec(memory_space=vmem), pl.BlockSpec(memory_space=vmem)),
        scratch_shapes=[
            pltpu.VMEM((n_keys, HEAD_DIM), jnp.float32),
            pltpu.VMEM((n_keys, HEAD_DIM), jnp.float32),
        ],
        cost_estimate=pl.CostEstimate(
            flops=flops,
            transcendentals=2 * rows * n_keys * heads,
            bytes_accessed=4 * rows * width * 2 + 4 * n_keys * HEAD_DIM * 2,
        ),
    )(q, do, keys, values, mq, mk)


def body(hidden, queries, grad_out, segment, key_proj, value_proj):
    tok_rows = hidden.shape[1]
    n_dp = lax.axis_size("dp")
    n_ctx = lax.axis_size("context")
    group = HEADS // KV_HEADS
    scale = HEAD_DIM ** (-0.5)
    width_kv = key_proj.shape[1]
    local_rows = hidden[0]

    ctx_canon = [("context", b) for b in reversed(range(_bits(n_ctx)))]
    dp_canon = [("dp", b) for b in reversed(range(_bits(n_dp)))]
    both_canon = dp_canon + ctx_canon

    def step(axis, bit):
        return (axis, n_dp if axis == "dp" else n_ctx, bit)

    ctx_far = [step("context", b) for b in reversed(range(_bits(n_ctx)))]
    dp_far = [step("dp", b) for b in reversed(range(_bits(n_dp)))]
    def interleave(first, second):
        out = []
        for k in range(max(len(first), len(second))):
            out += first[k:k + 1] + second[k:k + 1]
        return out

    order_a = ctx_far[:1] + interleave(ctx_far[1:-1], dp_far) + ctx_far[-1:]
    order_b = ctx_far[:1] + interleave(dp_far, ctx_far[1:-1]) + ctx_far[-1:]

    far_first = ctx_far[:1] + interleave(ctx_far[1:-1], dp_far) + ctx_far[-1:]
    proj = jnp.concatenate([key_proj, value_proj], axis=1)
    canonical = {("dp", b): n_ctx << b for b in range(_bits(n_dp))}
    canonical.update({("context", b): 1 << b for b in range(_bits(n_ctx))})
    canonical["origin"] = (("dp", n_ctx), ("context", 1))
    proj_all = pair_gather(proj[None], far_first, 1, canonical).reshape(-1, proj.shape[1])
    kv = jnp.dot(local_rows, proj_all, preferred_element_type=jnp.float32).astype(jnp.bfloat16)
    marks = segment[0].astype(jnp.bfloat16)
    marks_row = jnp.pad(marks, (0, 2 * HEAD_DIM - tok_rows))[None, :]
    kvm = jnp.concatenate([kv, marks_row], axis=0)[None]
    kvm_all = pair_gather(kvm, ctx_far, 0)
    keys = kvm_all[:, :tok_rows, :HEAD_DIM].reshape(-1, HEAD_DIM)
    values = kvm_all[:, :tok_rows, HEAD_DIM:].reshape(-1, HEAD_DIM)
    marks_all = kvm_all[:, tok_rows, :tok_rows].reshape(-1)

    mq = marks.astype(jnp.float32)[:, None]
    mk = marks_all.astype(jnp.float32)[None, :]
    grad_q, kv_part = attention_block(queries[0], grad_out[0], keys, values, mq, mk)
    kv_blocks = kv_part.reshape((2,) * len(ctx_far) + (tok_rows, kv_part.shape[1]))
    kv_grad = scatter_relative(kv_blocks, ctx_far).astype(jnp.bfloat16)

    dims_t = (((0,), (0,)), ((), ()))
    key_part = lax.dot_general(local_rows, kv_grad[:, :width_kv], dims_t, preferred_element_type=jnp.float32)
    value_part = lax.dot_general(local_rows, kv_grad[:, width_kv:], dims_t, preferred_element_type=jnp.float32)
    key_sum = scatter_sum(key_part.astype(jnp.bfloat16), order_a[::-1], both_canon, jnp.float32)
    value_sum = scatter_sum(value_part.astype(jnp.bfloat16), order_b[::-1], both_canon, jnp.float32)
    grad_queries = grad_q[None]
    return (grad_queries, key_sum, value_sum)


def solution(mesh):
    placed = (
        P("dp", "context", None),
        P("dp", "context", "head"),
        P("dp", "context", "head"),
        P("dp", "context"),
        P(("dp", "context"), "head"),
        P(("dp", "context"), "head"),
    )
    return jax.shard_map(
        body,
        mesh=mesh,
        in_specs=placed,
        out_specs=(
            P("dp", "context", "head"),
            P(("dp", "context"), "head"),
            P(("dp", "context"), "head"),
        ),
        check_vma=False,
    )
```

```python
import functools

import jax
import jax.numpy as jnp
from jax import lax
from jax.experimental import pallas as pl
from jax.experimental.pallas import tpu as pltpu
from jax.sharding import PartitionSpec as P

HEADS = 32
KV_HEADS = 8
HEAD_DIM = 128


far_below = -1e30


def _bits(n):
    return n.bit_length() - 1


def _exchange(x, axis, size, bit):
    perm = [(i, i ^ (1 << bit)) for i in range(size)]
    return lax.ppermute(x, axis, perm)


def _my_bit(axis, bit):
    return ((lax.axis_index(axis) >> bit) & 1) == 1


def gather_blocks(x, steps, canon):
    cur = x
    dims = []
    for axis, size, bit in steps:
        recv = _exchange(cur, axis, size, bit)
        mine = _my_bit(axis, bit)
        cur = jnp.where(mine, jnp.stack([recv, cur]), jnp.stack([cur, recv]))
        dims.insert(0, (axis, bit))
    order = [dims.index(c) for c in canon]
    cur = jnp.transpose(cur, order + list(range(len(dims), cur.ndim)))
    return cur.reshape((-1,) + x.shape[1:])


def scatter_sum(x, steps, canon, acc=None):
    nb = len(canon)
    acc = acc or x.dtype
    block = x.shape[0] >> nb
    cur = x.reshape((2,) * nb + (block,) + x.shape[1:])
    dims = list(canon)
    for axis, size, bit in steps:
        at = dims.index((axis, bit))
        lo = lax.index_in_dim(cur, 0, at, keepdims=False)
        hi = lax.index_in_dim(cur, 1, at, keepdims=False)
        mine = _my_bit(axis, bit)
        keep = jnp.where(mine, hi, lo)
        send = jnp.where(mine, lo, hi)
        total = keep.astype(acc) + _exchange(send, axis, size, bit).astype(acc)
        cur = total if len(dims) == 1 else total.astype(x.dtype)
        dims.pop(at)
    return cur


def gather_relative(x, steps):
    cur = x
    for axis, size, bit in steps:
        cur = jnp.stack([cur, _exchange(cur, axis, size, bit)])
    return cur


def scatter_relative(x, steps):
    dims = [bit for _, _, bit in steps][::-1]
    cur = x
    for axis, size, bit in steps[::-1]:
        at = dims.index(bit)
        keep = lax.index_in_dim(cur, 0, at, keepdims=False)
        send = lax.index_in_dim(cur, 1, at, keepdims=False)
        total = keep.astype(jnp.float32) + _exchange(send, axis, size, bit).astype(jnp.float32)
        cur = total if len(dims) == 1 else total.astype(x.dtype)
        dims.pop(at)
    return cur


def _gather_kernel(steps, canonical, x_ref, o_ref, held, send_sems, recv_sems, local_sem):
    mesh = pl.DeviceIdType.MESH
    partners = [{axis: lax.bitwise_xor(lax.axis_index(axis), 1 << bit)} for axis, _, bit in steps]
    barrier = pltpu.get_barrier_semaphore()
    for p in partners:
        pl.semaphore_signal(barrier, inc=1, device_id=p, device_id_type=mesh)
    pl.semaphore_wait(barrier, len(partners))
    local = pltpu.make_async_copy(x_ref, held.at[0:1], local_sem)
    local.start()
    sends = []

    def push(src, lo, hi, j):
        base = 1 << j
        copy = pltpu.make_async_remote_copy(
            src_ref=src,
            dst_ref=held.at[base + lo:base + hi],
            send_sem=send_sems.at[len(sends)],
            recv_sem=recv_sems.at[j],
            device_id=partners[j],
            device_id_type=mesh,
        )
        copy.start()
        sends.append(copy)

    for j in range(len(partners)):
        push(x_ref, 0, 1, j)
    for i in range(len(partners)):
        lo, hi = 1 << i, 2 << i
        arrived = pltpu.make_async_remote_copy(
            src_ref=held.at[lo:hi],
            dst_ref=held.at[lo:hi],
            send_sem=send_sems.at[0],
            recv_sem=recv_sems.at[i],
            device_id=partners[i],
            device_id_type=mesh,
        )
        arrived.wait_recv()
        for j in range(i + 1, len(partners)):
            push(held.at[lo:hi], lo, hi, j)
    for copy in sends:
        copy.wait_send()
    local.wait()
    if canonical is None:
        out = pltpu.make_async_copy(held, o_ref, local_sem)
        out.start()
        out.wait()
        return
    weights = []
    me = 0
    for axis, size, bit in steps:
        idx = lax.axis_index(axis)
        mine = (idx // (1 << bit)) % 2
        weights.append(canonical[(axis, bit)] * (1 - 2 * mine))
    for axis, stride in canonical["origin"]:
        me = me + lax.axis_index(axis) * stride
    for r in range(1 << len(steps)):
        at = me
        for k in range(len(steps)):
            if (r >> k) & 1:
                at = at + weights[k]
        pltpu.make_async_copy(held.at[r:r + 1], o_ref.at[pl.ds(at, 1)], local_sem).start()
    pltpu.make_async_copy(held, o_ref, local_sem).wait()


def pair_gather(x, steps, collective_id, canonical=None):
    n = 1 << len(steps)
    shape = (n,) + x.shape[1:]
    return pl.pallas_call(
        functools.partial(_gather_kernel, steps, canonical),
        out_shape=jax.ShapeDtypeStruct(shape, x.dtype),
        in_specs=[pl.BlockSpec(memory_space=pltpu.VMEM)],
        out_specs=pl.BlockSpec(memory_space=pltpu.VMEM),
        scratch_shapes=[
            pltpu.VMEM(shape, x.dtype),
            pltpu.SemaphoreType.DMA((len(steps) * (len(steps) + 1) // 2,)),
            pltpu.SemaphoreType.DMA((len(steps),)),
            pltpu.SemaphoreType.DMA,
        ],
        compiler_params=pltpu.CompilerParams(collective_id=collective_id, has_side_effects=True),
    )(x)


def _scatter_kernel(steps, x_ref, o_ref, acc, rbuf, sbuf, staged, send_sems, recv_sems, local_sem):
    mesh = pl.DeviceIdType.MESH
    partners = [{axis: lax.bitwise_xor(lax.axis_index(axis), 1 << bit)} for axis, _, bit in steps]
    barrier = pltpu.get_barrier_semaphore()
    for p in partners:
        pl.semaphore_signal(barrier, inc=1, device_id=p, device_id_type=mesh)
    pl.semaphore_wait(barrier, len(partners))
    for k in reversed(range(len(steps))):
        half = 1 << k
        off = half - 1
        if k == len(steps) - 1:
            src = x_ref.at[half:2 * half]
        else:
            sbuf[off:off + half] = acc[half:2 * half].astype(sbuf.dtype)
            stage = pltpu.make_async_copy(sbuf.at[off:off + half], staged.at[off:off + half], local_sem)
            stage.start()
            stage.wait()
            src = staged.at[off:off + half]
        copy = pltpu.make_async_remote_copy(
            src_ref=src,
            dst_ref=rbuf.at[off:off + half],
            send_sem=send_sems.at[k],
            recv_sem=recv_sems.at[k],
            device_id=partners[k],
            device_id_type=mesh,
        )
        copy.start()
        copy.wait()
        got = rbuf[off:off + half].astype(jnp.float32)
        if k == len(steps) - 1:
            acc[0:half] = x_ref[0:half].astype(jnp.float32) + got
        else:
            acc[0:half] = acc[0:half] + got
    o_ref[...] = acc[0]


def pair_scatter(x, steps, collective_id):
    n = x.shape[0]
    block = x.shape[1:]
    return pl.pallas_call(
        functools.partial(_scatter_kernel, steps),
        out_shape=jax.ShapeDtypeStruct(block, jnp.float32),
        in_specs=[pl.BlockSpec(memory_space=pltpu.VMEM)],
        out_specs=pl.BlockSpec(memory_space=pltpu.VMEM),
        scratch_shapes=[
            pltpu.VMEM((n // 2,) + block, jnp.float32),
            pltpu.VMEM((n - 1,) + block, x.dtype),
            pltpu.VMEM((n - 1,) + block, x.dtype),
            pltpu.VMEM((n - 1,) + block, x.dtype),
            pltpu.SemaphoreType.DMA((len(steps),)),
            pltpu.SemaphoreType.DMA((len(steps),)),
            pltpu.SemaphoreType.DMA,
        ],
        compiler_params=pltpu.CompilerParams(collective_id=collective_id, has_side_effects=True),
    )(x)


def _attention_kernel(q_ref, do_ref, k_ref, v_ref, mq_ref, mk_ref, gq_ref, dkv_ref, dk_acc, dv_acc):
    scale = HEAD_DIM ** (-0.5)
    keys = k_ref[...]
    values = v_ref[...]
    same = mq_ref[...] == mk_ref[...]
    dk_acc[...] = jnp.zeros_like(dk_acc)
    dv_acc[...] = jnp.zeros_like(dv_acc)
    nt = (((1,), (1,)), ((), ()))
    for h in range(q_ref.shape[1] // HEAD_DIM):
        cols = slice(h * HEAD_DIM, (h + 1) * HEAD_DIM)
        qh = q_ref[:, cols]
        doh = do_ref[:, cols]
        raw = lax.dot_general(qh, keys, nt, preferred_element_type=jnp.float32) * scale
        raw = jnp.where(same, raw, far_below)
        top = jnp.max(raw, axis=1, keepdims=True)
        total = jnp.sum(jnp.exp(raw - top), axis=1, keepdims=True)
        probs = jnp.exp(raw - (top + jnp.log(total)))
        probs_b = probs.astype(jnp.bfloat16)
        out = jnp.dot(probs_b, values, preferred_element_type=jnp.float32).astype(jnp.bfloat16)
        delta = jnp.sum(doh.astype(jnp.float32) * out.astype(jnp.float32), axis=1, keepdims=True)
        dv_acc[...] += jnp.dot(probs.T.astype(jnp.bfloat16), doh, preferred_element_type=jnp.float32)
        prob_grad = lax.dot_general(doh, values, nt, preferred_element_type=jnp.float32)
        dscores = probs * (prob_grad - delta)
        gq_ref[:, cols] = (
            jnp.dot(dscores.astype(jnp.bfloat16), keys, preferred_element_type=jnp.float32) * scale
        ).astype(gq_ref.dtype)
        dk_acc[...] += jnp.dot(
            dscores.T.astype(jnp.bfloat16), qh, preferred_element_type=jnp.float32
        ) * scale
    dkv_ref[:, :HEAD_DIM] = dk_acc[...].astype(dkv_ref.dtype)
    dkv_ref[:, HEAD_DIM:] = dv_acc[...].astype(dkv_ref.dtype)


def attention_block(q, do, keys, values, mq, mk):
    rows, width = q.shape
    n_keys = keys.shape[0]
    heads = width // HEAD_DIM
    flops = 2 * rows * n_keys * HEAD_DIM * heads * 6
    vmem = pltpu.VMEM
    return pl.pallas_call(
        _attention_kernel,
        out_shape=(
            jax.ShapeDtypeStruct((rows, width), jnp.bfloat16),
            jax.ShapeDtypeStruct((n_keys, 2 * HEAD_DIM), jnp.bfloat16),
        ),
        in_specs=[pl.BlockSpec(memory_space=vmem)] * 6,
        out_specs=(pl.BlockSpec(memory_space=vmem), pl.BlockSpec(memory_space=vmem)),
        scratch_shapes=[
            pltpu.VMEM((n_keys, HEAD_DIM), jnp.float32),
            pltpu.VMEM((n_keys, HEAD_DIM), jnp.float32),
        ],
        cost_estimate=pl.CostEstimate(
            flops=flops,
            transcendentals=2 * rows * n_keys * heads,
            bytes_accessed=4 * rows * width * 2 + 4 * n_keys * HEAD_DIM * 2,
        ),
    )(q, do, keys, values, mq, mk)


def body(hidden, queries, grad_out, segment, key_proj, value_proj):
    tok_rows = hidden.shape[1]
    n_dp = lax.axis_size("dp")
    n_ctx = lax.axis_size("context")
    group = HEADS // KV_HEADS
    scale = HEAD_DIM ** (-0.5)
    width_kv = key_proj.shape[1]
    local_rows = hidden[0]

    ctx_canon = [("context", b) for b in reversed(range(_bits(n_ctx)))]
    dp_canon = [("dp", b) for b in reversed(range(_bits(n_dp)))]
    both_canon = dp_canon + ctx_canon

    def step(axis, bit):
        return (axis, n_dp if axis == "dp" else n_ctx, bit)

    ctx_far = [step("context", b) for b in reversed(range(_bits(n_ctx)))]
    dp_far = [step("dp", b) for b in reversed(range(_bits(n_dp)))]
    def interleave(first, second):
        out = []
        for k in range(max(len(first), len(second))):
            out += first[k:k + 1] + second[k:k + 1]
        return out

    order_a = ctx_far[:1] + interleave(ctx_far[1:-1], dp_far) + ctx_far[-1:]
    order_b = ctx_far[:1] + interleave(dp_far, ctx_far[1:-1]) + ctx_far[-1:]

    far_first = ctx_far[:1] + interleave(ctx_far[1:-1], dp_far) + ctx_far[-1:]
    proj = jnp.concatenate([key_proj, value_proj], axis=1)
    canonical = {("dp", b): n_ctx << b for b in range(_bits(n_dp))}
    canonical.update({("context", b): 1 << b for b in range(_bits(n_ctx))})
    canonical["origin"] = (("dp", n_ctx), ("context", 1))
    proj_all = pair_gather(proj[None], far_first, 1, canonical).reshape(-1, proj.shape[1])
    kv = jnp.dot(local_rows, proj_all, preferred_element_type=jnp.float32).astype(jnp.bfloat16)
    marks = segment[0].astype(jnp.bfloat16)
    marks_row = jnp.pad(marks, (0, 2 * HEAD_DIM - tok_rows))[None, :]
    kvm = jnp.concatenate([kv, marks_row], axis=0)[None]
    kvm_all = pair_gather(kvm, ctx_far, 0)
    keys = kvm_all[:, :tok_rows, :HEAD_DIM].reshape(-1, HEAD_DIM)
    values = kvm_all[:, :tok_rows, HEAD_DIM:].reshape(-1, HEAD_DIM)
    marks_all = kvm_all[:, tok_rows, :tok_rows].reshape(-1)

    mq = marks.astype(jnp.float32)[:, None]
    mk = marks_all.astype(jnp.float32)[None, :]
    grad_q, kv_part = attention_block(queries[0], grad_out[0], keys, values, mq, mk)
    kv_blocks = kv_part.reshape((-1, tok_rows, kv_part.shape[1]))
    kv_grad = pair_scatter(kv_blocks, ctx_far, 2).astype(jnp.bfloat16)

    dims_t = (((0,), (0,)), ((), ()))
    key_part = lax.dot_general(local_rows, kv_grad[:, :width_kv], dims_t, preferred_element_type=jnp.float32)
    value_part = lax.dot_general(local_rows, kv_grad[:, width_kv:], dims_t, preferred_element_type=jnp.float32)
    key_sum = scatter_sum(key_part.astype(jnp.bfloat16), order_a[::-1], both_canon, jnp.float32)
    value_sum = scatter_sum(value_part.astype(jnp.bfloat16), order_b[::-1], both_canon, jnp.float32)
    grad_queries = grad_q[None]
    return (grad_queries, key_sum, value_sum)


def solution(mesh):
    placed = (
        P("dp", "context", None),
        P("dp", "context", "head"),
        P("dp", "context", "head"),
        P("dp", "context"),
        P(("dp", "context"), "head"),
        P(("dp", "context"), "head"),
    )
    return jax.shard_map(
        body,
        mesh=mesh,
        in_specs=placed,
        out_specs=(
            P("dp", "context", "head"),
            P(("dp", "context"), "head"),
            P(("dp", "context"), "head"),
        ),
        check_vma=False,
    )
```

```python
import functools

import jax
import jax.numpy as jnp
from jax import lax
from jax.experimental import pallas as pl
from jax.experimental.pallas import tpu as pltpu
from jax.sharding import PartitionSpec as P

HEADS = 32
KV_HEADS = 8
HEAD_DIM = 128


far_below = -1e30


def _bits(n):
    return n.bit_length() - 1


def _exchange(x, axis, size, bit):
    perm = [(i, i ^ (1 << bit)) for i in range(size)]
    return lax.ppermute(x, axis, perm)


def _my_bit(axis, bit):
    return ((lax.axis_index(axis) >> bit) & 1) == 1


def gather_blocks(x, steps, canon):
    cur = x
    dims = []
    for axis, size, bit in steps:
        recv = _exchange(cur, axis, size, bit)
        mine = _my_bit(axis, bit)
        cur = jnp.where(mine, jnp.stack([recv, cur]), jnp.stack([cur, recv]))
        dims.insert(0, (axis, bit))
    order = [dims.index(c) for c in canon]
    cur = jnp.transpose(cur, order + list(range(len(dims), cur.ndim)))
    return cur.reshape((-1,) + x.shape[1:])


def scatter_sum(x, steps, canon, acc=None):
    nb = len(canon)
    acc = acc or x.dtype
    block = x.shape[0] >> nb
    cur = x.reshape((2,) * nb + (block,) + x.shape[1:])
    dims = list(canon)
    for axis, size, bit in steps:
        at = dims.index((axis, bit))
        lo = lax.index_in_dim(cur, 0, at, keepdims=False)
        hi = lax.index_in_dim(cur, 1, at, keepdims=False)
        mine = _my_bit(axis, bit)
        keep = jnp.where(mine, hi, lo)
        send = jnp.where(mine, lo, hi)
        total = keep.astype(acc) + _exchange(send, axis, size, bit).astype(acc)
        cur = total if len(dims) == 1 else total.astype(x.dtype)
        dims.pop(at)
    return cur


def gather_relative(x, steps):
    cur = x
    for axis, size, bit in steps:
        cur = jnp.stack([cur, _exchange(cur, axis, size, bit)])
    return cur


def scatter_relative(x, steps):
    dims = [bit for _, _, bit in steps][::-1]
    cur = x
    for axis, size, bit in steps[::-1]:
        at = dims.index(bit)
        keep = lax.index_in_dim(cur, 0, at, keepdims=False)
        send = lax.index_in_dim(cur, 1, at, keepdims=False)
        total = keep.astype(jnp.float32) + _exchange(send, axis, size, bit).astype(jnp.float32)
        cur = total if len(dims) == 1 else total.astype(x.dtype)
        dims.pop(at)
    return cur


def _gather_kernel(steps, canonical, x_ref, o_ref, held, send_sems, recv_sems, local_sem):
    mesh = pl.DeviceIdType.MESH
    partners = [{axis: lax.bitwise_xor(lax.axis_index(axis), 1 << bit)} for axis, _, bit in steps]
    barrier = pltpu.get_barrier_semaphore()
    for p in partners:
        pl.semaphore_signal(barrier, inc=1, device_id=p, device_id_type=mesh)
    pl.semaphore_wait(barrier, len(partners))
    local = pltpu.make_async_copy(x_ref, held.at[0:1], local_sem)
    local.start()
    sends = []

    def push(src, lo, hi, j):
        base = 1 << j
        copy = pltpu.make_async_remote_copy(
            src_ref=src,
            dst_ref=held.at[base + lo:base + hi],
            send_sem=send_sems.at[len(sends)],
            recv_sem=recv_sems.at[j],
            device_id=partners[j],
            device_id_type=mesh,
        )
        copy.start()
        sends.append(copy)

    for j in range(len(partners)):
        push(x_ref, 0, 1, j)
    for i in range(len(partners)):
        lo, hi = 1 << i, 2 << i
        arrived = pltpu.make_async_remote_copy(
            src_ref=held.at[lo:hi],
            dst_ref=held.at[lo:hi],
            send_sem=send_sems.at[0],
            recv_sem=recv_sems.at[i],
            device_id=partners[i],
            device_id_type=mesh,
        )
        arrived.wait_recv()
        for j in range(i + 1, len(partners)):
            push(held.at[lo:hi], lo, hi, j)
    for copy in sends:
        copy.wait_send()
    local.wait()
    if canonical is None:
        out = pltpu.make_async_copy(held, o_ref, local_sem)
        out.start()
        out.wait()
        return
    weights = []
    me = 0
    for axis, size, bit in steps:
        idx = lax.axis_index(axis)
        mine = (idx // (1 << bit)) % 2
        weights.append(canonical[(axis, bit)] * (1 - 2 * mine))
    for axis, stride in canonical["origin"]:
        me = me + lax.axis_index(axis) * stride
    for r in range(1 << len(steps)):
        at = me
        for k in range(len(steps)):
            if (r >> k) & 1:
                at = at + weights[k]
        pltpu.make_async_copy(held.at[r:r + 1], o_ref.at[pl.ds(at, 1)], local_sem).start()
    pltpu.make_async_copy(held, o_ref, local_sem).wait()


def pair_gather(x, steps, collective_id, canonical=None):
    n = 1 << len(steps)
    shape = (n,) + x.shape[1:]
    return pl.pallas_call(
        functools.partial(_gather_kernel, steps, canonical),
        out_shape=jax.ShapeDtypeStruct(shape, x.dtype),
        in_specs=[pl.BlockSpec(memory_space=pltpu.VMEM)],
        out_specs=pl.BlockSpec(memory_space=pltpu.VMEM),
        scratch_shapes=[
            pltpu.VMEM(shape, x.dtype),
            pltpu.SemaphoreType.DMA((len(steps) * (len(steps) + 1) // 2,)),
            pltpu.SemaphoreType.DMA((len(steps),)),
            pltpu.SemaphoreType.DMA,
        ],
        compiler_params=pltpu.CompilerParams(collective_id=collective_id, has_side_effects=True),
    )(x)


def _scatter_kernel(steps, canonical, x_in, o_ref, acc, rbuf, sbuf, staged, rel, send_sems, recv_sems, local_sem):
    mesh = pl.DeviceIdType.MESH
    partners = [{axis: lax.bitwise_xor(lax.axis_index(axis), 1 << bit)} for axis, _, bit in steps]
    x_ref = x_in
    if canonical is not None:
        weights = []
        me = 0
        for axis, size, bit in steps:
            mine = (lax.axis_index(axis) // (1 << bit)) % 2
            weights.append(canonical[(axis, bit)] * (1 - 2 * mine))
        for axis, stride in canonical["origin"]:
            me = me + lax.axis_index(axis) * stride
        for r in range(1 << len(steps)):
            at = me
            for k in range(len(steps)):
                if (r >> k) & 1:
                    at = at + weights[k]
            pltpu.make_async_copy(x_in.at[pl.ds(at, 1)], rel.at[r:r + 1], local_sem).start()
        pltpu.make_async_copy(x_in, rel, local_sem).wait()
        x_ref = rel
    barrier = pltpu.get_barrier_semaphore()
    for p in partners:
        pl.semaphore_signal(barrier, inc=1, device_id=p, device_id_type=mesh)
    pl.semaphore_wait(barrier, len(partners))
    for k in reversed(range(len(steps))):
        half = 1 << k
        off = half - 1
        if k == len(steps) - 1:
            src = x_ref.at[half:2 * half]
        else:
            sbuf[off:off + half] = acc[half:2 * half].astype(sbuf.dtype)
            stage = pltpu.make_async_copy(sbuf.at[off:off + half], staged.at[off:off + half], local_sem)
            stage.start()
            stage.wait()
            src = staged.at[off:off + half]
        copy = pltpu.make_async_remote_copy(
            src_ref=src,
            dst_ref=rbuf.at[off:off + half],
            send_sem=send_sems.at[k],
            recv_sem=recv_sems.at[k],
            device_id=partners[k],
            device_id_type=mesh,
        )
        copy.start()
        copy.wait()
        got = rbuf[off:off + half].astype(jnp.float32)
        if k == len(steps) - 1:
            acc[0:half] = x_ref[0:half].astype(jnp.float32) + got
        else:
            acc[0:half] = acc[0:half] + got
    o_ref[...] = acc[0]


def pair_scatter(x, steps, collective_id, canonical=None):
    n = x.shape[0]
    block = x.shape[1:]
    return pl.pallas_call(
        functools.partial(_scatter_kernel, steps, canonical),
        out_shape=jax.ShapeDtypeStruct(block, jnp.float32),
        in_specs=[pl.BlockSpec(memory_space=pltpu.VMEM)],
        out_specs=pl.BlockSpec(memory_space=pltpu.VMEM),
        scratch_shapes=[
            pltpu.VMEM((n // 2,) + block, jnp.float32),
            pltpu.VMEM((n - 1,) + block, x.dtype),
            pltpu.VMEM((n - 1,) + block, x.dtype),
            pltpu.VMEM((n - 1,) + block, x.dtype),
            pltpu.VMEM((n if canonical else 1,) + block, x.dtype),
            pltpu.SemaphoreType.DMA((len(steps),)),
            pltpu.SemaphoreType.DMA((len(steps),)),
            pltpu.SemaphoreType.DMA,
        ],
        compiler_params=pltpu.CompilerParams(collective_id=collective_id, has_side_effects=True),
    )(x)


def _attention_kernel(q_ref, do_ref, k_ref, v_ref, mq_ref, mk_ref, gq_ref, dkv_ref, dk_acc, dv_acc):
    scale = HEAD_DIM ** (-0.5)
    keys = k_ref[...]
    values = v_ref[...]
    same = mq_ref[...] == mk_ref[...]
    dk_acc[...] = jnp.zeros_like(dk_acc)
    dv_acc[...] = jnp.zeros_like(dv_acc)
    nt = (((1,), (1,)), ((), ()))
    for h in range(q_ref.shape[1] // HEAD_DIM):
        cols = slice(h * HEAD_DIM, (h + 1) * HEAD_DIM)
        qh = q_ref[:, cols]
        doh = do_ref[:, cols]
        raw = lax.dot_general(qh, keys, nt, preferred_element_type=jnp.float32) * scale
        raw = jnp.where(same, raw, far_below)
        top = jnp.max(raw, axis=1, keepdims=True)
        total = jnp.sum(jnp.exp(raw - top), axis=1, keepdims=True)
        probs = jnp.exp(raw - (top + jnp.log(total)))
        probs_b = probs.astype(jnp.bfloat16)
        out = jnp.dot(probs_b, values, preferred_element_type=jnp.float32).astype(jnp.bfloat16)
        delta = jnp.sum(doh.astype(jnp.float32) * out.astype(jnp.float32), axis=1, keepdims=True)
        dv_acc[...] += jnp.dot(probs.T.astype(jnp.bfloat16), doh, preferred_element_type=jnp.float32)
        prob_grad = lax.dot_general(doh, values, nt, preferred_element_type=jnp.float32)
        dscores = probs * (prob_grad - delta)
        gq_ref[:, cols] = (
            jnp.dot(dscores.astype(jnp.bfloat16), keys, preferred_element_type=jnp.float32) * scale
        ).astype(gq_ref.dtype)
        dk_acc[...] += jnp.dot(
            dscores.T.astype(jnp.bfloat16), qh, preferred_element_type=jnp.float32
        ) * scale
    dkv_ref[:, :HEAD_DIM] = dk_acc[...].astype(dkv_ref.dtype)
    dkv_ref[:, HEAD_DIM:] = dv_acc[...].astype(dkv_ref.dtype)


def attention_block(q, do, keys, values, mq, mk):
    rows, width = q.shape
    n_keys = keys.shape[0]
    heads = width // HEAD_DIM
    flops = 2 * rows * n_keys * HEAD_DIM * heads * 6
    vmem = pltpu.VMEM
    return pl.pallas_call(
        _attention_kernel,
        out_shape=(
            jax.ShapeDtypeStruct((rows, width), jnp.bfloat16),
            jax.ShapeDtypeStruct((n_keys, 2 * HEAD_DIM), jnp.bfloat16),
        ),
        in_specs=[pl.BlockSpec(memory_space=vmem)] * 6,
        out_specs=(pl.BlockSpec(memory_space=vmem), pl.BlockSpec(memory_space=vmem)),
        scratch_shapes=[
            pltpu.VMEM((n_keys, HEAD_DIM), jnp.float32),
            pltpu.VMEM((n_keys, HEAD_DIM), jnp.float32),
        ],
        cost_estimate=pl.CostEstimate(
            flops=flops,
            transcendentals=2 * rows * n_keys * heads,
            bytes_accessed=4 * rows * width * 2 + 4 * n_keys * HEAD_DIM * 2,
        ),
    )(q, do, keys, values, mq, mk)


def body(hidden, queries, grad_out, segment, key_proj, value_proj):
    tok_rows = hidden.shape[1]
    n_dp = lax.axis_size("dp")
    n_ctx = lax.axis_size("context")
    group = HEADS // KV_HEADS
    scale = HEAD_DIM ** (-0.5)
    width_kv = key_proj.shape[1]
    local_rows = hidden[0]

    ctx_canon = [("context", b) for b in reversed(range(_bits(n_ctx)))]
    dp_canon = [("dp", b) for b in reversed(range(_bits(n_dp)))]
    both_canon = dp_canon + ctx_canon

    def step(axis, bit):
        return (axis, n_dp if axis == "dp" else n_ctx, bit)

    ctx_far = [step("context", b) for b in reversed(range(_bits(n_ctx)))]
    dp_far = [step("dp", b) for b in reversed(range(_bits(n_dp)))]
    def interleave(first, second):
        out = []
        for k in range(max(len(first), len(second))):
            out += first[k:k + 1] + second[k:k + 1]
        return out

    order_a = ctx_far[:1] + interleave(ctx_far[1:-1], dp_far) + ctx_far[-1:]
    order_b = ctx_far[:1] + interleave(dp_far, ctx_far[1:-1]) + ctx_far[-1:]

    far_first = ctx_far[:1] + interleave(ctx_far[1:-1], dp_far) + ctx_far[-1:]
    proj = jnp.concatenate([key_proj, value_proj], axis=1)
    canonical = {("dp", b): n_ctx << b for b in range(_bits(n_dp))}
    canonical.update({("context", b): 1 << b for b in range(_bits(n_ctx))})
    canonical["origin"] = (("dp", n_ctx), ("context", 1))
    proj_all = pair_gather(proj[None], far_first, 1, canonical).reshape(-1, proj.shape[1])
    kv = jnp.dot(local_rows, proj_all, preferred_element_type=jnp.float32).astype(jnp.bfloat16)
    marks = segment[0].astype(jnp.bfloat16)
    marks_row = jnp.pad(marks, (0, 2 * HEAD_DIM - tok_rows))[None, :]
    kvm = jnp.concatenate([kv, marks_row], axis=0)[None]
    kvm_all = pair_gather(kvm, ctx_far, 0)
    keys = kvm_all[:, :tok_rows, :HEAD_DIM].reshape(-1, HEAD_DIM)
    values = kvm_all[:, :tok_rows, HEAD_DIM:].reshape(-1, HEAD_DIM)
    marks_all = kvm_all[:, tok_rows, :tok_rows].reshape(-1)

    mq = marks.astype(jnp.float32)[:, None]
    mk = marks_all.astype(jnp.float32)[None, :]
    grad_q, kv_part = attention_block(queries[0], grad_out[0], keys, values, mq, mk)
    kv_blocks = kv_part.reshape((-1, tok_rows, kv_part.shape[1]))
    kv_grad = pair_scatter(kv_blocks, ctx_far, 2).astype(jnp.bfloat16)

    dims_t = (((0,), (0,)), ((), ()))
    key_part = lax.dot_general(local_rows, kv_grad[:, :width_kv], dims_t, preferred_element_type=jnp.float32)
    value_part = lax.dot_general(local_rows, kv_grad[:, width_kv:], dims_t, preferred_element_type=jnp.float32)
    parts = jnp.concatenate([key_part, value_part], axis=1).astype(jnp.bfloat16)
    parts = parts.reshape((-1, key_proj.shape[0], parts.shape[1]))
    summed = pair_scatter(parts, far_first, 3, canonical)
    key_sum, value_sum = summed[:, :width_kv], summed[:, width_kv:]
    grad_queries = grad_q[None]
    return (grad_queries, key_sum, value_sum)


def solution(mesh):
    placed = (
        P("dp", "context", None),
        P("dp", "context", "head"),
        P("dp", "context", "head"),
        P("dp", "context"),
        P(("dp", "context"), "head"),
        P(("dp", "context"), "head"),
    )
    return jax.shard_map(
        body,
        mesh=mesh,
        in_specs=placed,
        out_specs=(
            P("dp", "context", "head"),
            P(("dp", "context"), "head"),
            P(("dp", "context"), "head"),
        ),
        check_vma=False,
    )
```

```python
import functools

import jax
import jax.numpy as jnp
from jax import lax
from jax.experimental import pallas as pl
from jax.experimental.pallas import tpu as pltpu
from jax.sharding import PartitionSpec as P

HEADS = 32
KV_HEADS = 8
HEAD_DIM = 128


far_below = -1e30


def _bits(n):
    return n.bit_length() - 1


def _exchange(x, axis, size, bit):
    perm = [(i, i ^ (1 << bit)) for i in range(size)]
    return lax.ppermute(x, axis, perm)


def _my_bit(axis, bit):
    return ((lax.axis_index(axis) >> bit) & 1) == 1


def gather_blocks(x, steps, canon):
    cur = x
    dims = []
    for axis, size, bit in steps:
        recv = _exchange(cur, axis, size, bit)
        mine = _my_bit(axis, bit)
        cur = jnp.where(mine, jnp.stack([recv, cur]), jnp.stack([cur, recv]))
        dims.insert(0, (axis, bit))
    order = [dims.index(c) for c in canon]
    cur = jnp.transpose(cur, order + list(range(len(dims), cur.ndim)))
    return cur.reshape((-1,) + x.shape[1:])


def scatter_sum(x, steps, canon, acc=None):
    nb = len(canon)
    acc = acc or x.dtype
    block = x.shape[0] >> nb
    cur = x.reshape((2,) * nb + (block,) + x.shape[1:])
    dims = list(canon)
    for axis, size, bit in steps:
        at = dims.index((axis, bit))
        lo = lax.index_in_dim(cur, 0, at, keepdims=False)
        hi = lax.index_in_dim(cur, 1, at, keepdims=False)
        mine = _my_bit(axis, bit)
        keep = jnp.where(mine, hi, lo)
        send = jnp.where(mine, lo, hi)
        total = keep.astype(acc) + _exchange(send, axis, size, bit).astype(acc)
        cur = total if len(dims) == 1 else total.astype(x.dtype)
        dims.pop(at)
    return cur


def gather_relative(x, steps):
    cur = x
    for axis, size, bit in steps:
        cur = jnp.stack([cur, _exchange(cur, axis, size, bit)])
    return cur


def scatter_relative(x, steps):
    dims = [bit for _, _, bit in steps][::-1]
    cur = x
    for axis, size, bit in steps[::-1]:
        at = dims.index(bit)
        keep = lax.index_in_dim(cur, 0, at, keepdims=False)
        send = lax.index_in_dim(cur, 1, at, keepdims=False)
        total = keep.astype(jnp.float32) + _exchange(send, axis, size, bit).astype(jnp.float32)
        cur = total if len(dims) == 1 else total.astype(x.dtype)
        dims.pop(at)
    return cur


def _gather_kernel(steps, canonical, x_ref, o_ref, held, send_sems, recv_sems, local_sem):
    mesh = pl.DeviceIdType.MESH
    partners = [{axis: lax.bitwise_xor(lax.axis_index(axis), 1 << bit)} for axis, _, bit in steps]
    barrier = pltpu.get_barrier_semaphore()
    for p in partners:
        pl.semaphore_signal(barrier, inc=1, device_id=p, device_id_type=mesh)
    pl.semaphore_wait(barrier, len(partners))
    local = pltpu.make_async_copy(x_ref, held.at[0:1], local_sem)
    local.start()
    sends = []

    def push(src, lo, hi, j):
        base = 1 << j
        copy = pltpu.make_async_remote_copy(
            src_ref=src,
            dst_ref=held.at[base + lo:base + hi],
            send_sem=send_sems.at[len(sends)],
            recv_sem=recv_sems.at[j],
            device_id=partners[j],
            device_id_type=mesh,
        )
        copy.start()
        sends.append(copy)

    for j in range(len(partners)):
        push(x_ref, 0, 1, j)
    for i in range(len(partners)):
        lo, hi = 1 << i, 2 << i
        arrived = pltpu.make_async_remote_copy(
            src_ref=held.at[lo:hi],
            dst_ref=held.at[lo:hi],
            send_sem=send_sems.at[0],
            recv_sem=recv_sems.at[i],
            device_id=partners[i],
            device_id_type=mesh,
        )
        arrived.wait_recv()
        for j in range(i + 1, len(partners)):
            push(held.at[lo:hi], lo, hi, j)
    for copy in sends:
        copy.wait_send()
    local.wait()
    if canonical is None:
        out = pltpu.make_async_copy(held, o_ref, local_sem)
        out.start()
        out.wait()
        return
    weights = []
    me = 0
    for axis, size, bit in steps:
        idx = lax.axis_index(axis)
        mine = (idx // (1 << bit)) % 2
        weights.append(canonical[(axis, bit)] * (1 - 2 * mine))
    for axis, stride in canonical["origin"]:
        me = me + lax.axis_index(axis) * stride
    for r in range(1 << len(steps)):
        at = me
        for k in range(len(steps)):
            if (r >> k) & 1:
                at = at + weights[k]
        pltpu.make_async_copy(held.at[r:r + 1], o_ref.at[pl.ds(at, 1)], local_sem).start()
    pltpu.make_async_copy(held, o_ref, local_sem).wait()


def pair_gather(x, steps, collective_id, canonical=None):
    n = 1 << len(steps)
    shape = (n,) + x.shape[1:]
    return pl.pallas_call(
        functools.partial(_gather_kernel, steps, canonical),
        out_shape=jax.ShapeDtypeStruct(shape, x.dtype),
        in_specs=[pl.BlockSpec(memory_space=pltpu.VMEM)],
        out_specs=pl.BlockSpec(memory_space=pltpu.VMEM),
        scratch_shapes=[
            pltpu.VMEM(shape, x.dtype),
            pltpu.SemaphoreType.DMA((len(steps) * (len(steps) + 1) // 2,)),
            pltpu.SemaphoreType.DMA((len(steps),)),
            pltpu.SemaphoreType.DMA,
        ],
        compiler_params=pltpu.CompilerParams(collective_id=collective_id, has_side_effects=True),
    )(x)


def _scatter_kernel(steps, canonical, x_in, o_ref, acc, rbuf, sbuf, staged, rel, send_sems, recv_sems, local_sem):
    mesh = pl.DeviceIdType.MESH
    partners = [{axis: lax.bitwise_xor(lax.axis_index(axis), 1 << bit)} for axis, _, bit in steps]
    x_ref = x_in
    if canonical is not None:
        weights = []
        me = 0
        for axis, size, bit in steps:
            mine = (lax.axis_index(axis) // (1 << bit)) % 2
            weights.append(canonical[(axis, bit)] * (1 - 2 * mine))
        for axis, stride in canonical["origin"]:
            me = me + lax.axis_index(axis) * stride
        for r in range(1 << len(steps)):
            at = me
            for k in range(len(steps)):
                if (r >> k) & 1:
                    at = at + weights[k]
            pltpu.make_async_copy(x_in.at[pl.ds(at, 1)], rel.at[r:r + 1], local_sem).start()
        pltpu.make_async_copy(x_in, rel, local_sem).wait()
        x_ref = rel
    barrier = pltpu.get_barrier_semaphore()
    for p in partners:
        pl.semaphore_signal(barrier, inc=1, device_id=p, device_id_type=mesh)
    pl.semaphore_wait(barrier, len(partners))
    for k in reversed(range(len(steps))):
        half = 1 << k
        off = half - 1
        if k == len(steps) - 1:
            src = x_ref.at[half:2 * half]
        else:
            sbuf[off:off + half] = acc[half:2 * half].astype(sbuf.dtype)
            stage = pltpu.make_async_copy(sbuf.at[off:off + half], staged.at[off:off + half], local_sem)
            stage.start()
            stage.wait()
            src = staged.at[off:off + half]
        copy = pltpu.make_async_remote_copy(
            src_ref=src,
            dst_ref=rbuf.at[off:off + half],
            send_sem=send_sems.at[k],
            recv_sem=recv_sems.at[k],
            device_id=partners[k],
            device_id_type=mesh,
        )
        copy.start()
        copy.wait()
        got = rbuf[off:off + half].astype(jnp.float32)
        if k == len(steps) - 1:
            acc[0:half] = x_ref[0:half].astype(jnp.float32) + got
        else:
            acc[0:half] = acc[0:half] + got
    o_ref[...] = acc[0]


def pair_scatter(x, steps, collective_id, canonical=None):
    n = x.shape[0]
    block = x.shape[1:]
    return pl.pallas_call(
        functools.partial(_scatter_kernel, steps, canonical),
        out_shape=jax.ShapeDtypeStruct(block, jnp.float32),
        in_specs=[pl.BlockSpec(memory_space=pltpu.VMEM)],
        out_specs=pl.BlockSpec(memory_space=pltpu.VMEM),
        scratch_shapes=[
            pltpu.VMEM((n // 2,) + block, jnp.float32),
            pltpu.VMEM((n - 1,) + block, x.dtype),
            pltpu.VMEM((n - 1,) + block, x.dtype),
            pltpu.VMEM((n - 1,) + block, x.dtype),
            pltpu.VMEM((n if canonical else 1,) + block, x.dtype),
            pltpu.SemaphoreType.DMA((len(steps),)),
            pltpu.SemaphoreType.DMA((len(steps),)),
            pltpu.SemaphoreType.DMA,
        ],
        compiler_params=pltpu.CompilerParams(collective_id=collective_id, has_side_effects=True),
    )(x)


def _attention_kernel(q_ref, do_ref, k_ref, v_ref, mq_ref, mk_ref, gq_ref, dkv_ref, dk_acc, dv_acc):
    scale = HEAD_DIM ** (-0.5)
    keys = k_ref[...]
    values = v_ref[...]
    same = mq_ref[...] == mk_ref[...]
    dk_acc[...] = jnp.zeros_like(dk_acc)
    dv_acc[...] = jnp.zeros_like(dv_acc)
    nt = (((1,), (1,)), ((), ()))
    for h in range(q_ref.shape[1] // HEAD_DIM):
        cols = slice(h * HEAD_DIM, (h + 1) * HEAD_DIM)
        qh = q_ref[:, cols]
        doh = do_ref[:, cols]
        raw = lax.dot_general(qh, keys, nt, preferred_element_type=jnp.float32) * scale
        raw = jnp.where(same, raw, far_below)
        top = jnp.max(raw, axis=1, keepdims=True)
        total = jnp.sum(jnp.exp(raw - top), axis=1, keepdims=True)
        probs = jnp.exp(raw - (top + jnp.log(total)))
        probs_b = probs.astype(jnp.bfloat16)
        out = jnp.dot(probs_b, values, preferred_element_type=jnp.float32).astype(jnp.bfloat16)
        delta = jnp.sum(doh.astype(jnp.float32) * out.astype(jnp.float32), axis=1, keepdims=True)
        dv_acc[...] += jnp.dot(probs.T.astype(jnp.bfloat16), doh, preferred_element_type=jnp.float32)
        prob_grad = lax.dot_general(doh, values, nt, preferred_element_type=jnp.float32)
        dscores = probs * (prob_grad - delta)
        gq_ref[:, cols] = (
            jnp.dot(dscores.astype(jnp.bfloat16), keys, preferred_element_type=jnp.float32) * scale
        ).astype(gq_ref.dtype)
        dk_acc[...] += jnp.dot(
            dscores.T.astype(jnp.bfloat16), qh, preferred_element_type=jnp.float32
        ) * scale
    dkv_ref[:, :HEAD_DIM] = dk_acc[...].astype(dkv_ref.dtype)
    dkv_ref[:, HEAD_DIM:] = dv_acc[...].astype(dkv_ref.dtype)


def attention_block(q, do, keys, values, mq, mk):
    rows, width = q.shape
    n_keys = keys.shape[0]
    heads = width // HEAD_DIM
    flops = 2 * rows * n_keys * HEAD_DIM * heads * 6
    vmem = pltpu.VMEM
    return pl.pallas_call(
        _attention_kernel,
        out_shape=(
            jax.ShapeDtypeStruct((rows, width), jnp.bfloat16),
            jax.ShapeDtypeStruct((n_keys, 2 * HEAD_DIM), jnp.bfloat16),
        ),
        in_specs=[pl.BlockSpec(memory_space=vmem)] * 6,
        out_specs=(pl.BlockSpec(memory_space=vmem), pl.BlockSpec(memory_space=vmem)),
        scratch_shapes=[
            pltpu.VMEM((n_keys, HEAD_DIM), jnp.float32),
            pltpu.VMEM((n_keys, HEAD_DIM), jnp.float32),
        ],
        cost_estimate=pl.CostEstimate(
            flops=flops,
            transcendentals=2 * rows * n_keys * heads,
            bytes_accessed=4 * rows * width * 2 + 4 * n_keys * HEAD_DIM * 2,
        ),
    )(q, do, keys, values, mq, mk)


def body(hidden, queries, grad_out, segment, key_proj, value_proj):
    tok_rows = hidden.shape[1]
    n_dp = lax.axis_size("dp")
    n_ctx = lax.axis_size("context")
    group = HEADS // KV_HEADS
    scale = HEAD_DIM ** (-0.5)
    width_kv = key_proj.shape[1]
    local_rows = hidden[0]

    ctx_canon = [("context", b) for b in reversed(range(_bits(n_ctx)))]
    dp_canon = [("dp", b) for b in reversed(range(_bits(n_dp)))]
    both_canon = dp_canon + ctx_canon

    def step(axis, bit):
        return (axis, n_dp if axis == "dp" else n_ctx, bit)

    ctx_far = [step("context", b) for b in reversed(range(_bits(n_ctx)))]
    dp_far = [step("dp", b) for b in reversed(range(_bits(n_dp)))]
    def interleave(first, second):
        out = []
        for k in range(max(len(first), len(second))):
            out += first[k:k + 1] + second[k:k + 1]
        return out

    order_a = ctx_far[:1] + interleave(ctx_far[1:-1], dp_far) + ctx_far[-1:]
    order_b = ctx_far[:1] + interleave(dp_far, ctx_far[1:-1]) + ctx_far[-1:]

    far_first = ctx_far[:1] + interleave(ctx_far[1:-1], dp_far) + ctx_far[-1:]
    proj = jnp.concatenate([key_proj, value_proj], axis=1)
    canonical = {("dp", b): n_ctx << b for b in range(_bits(n_dp))}
    canonical.update({("context", b): 1 << b for b in range(_bits(n_ctx))})
    canonical["origin"] = (("dp", n_ctx), ("context", 1))
    proj_all = pair_gather(proj[None], far_first, 1, canonical).reshape(-1, proj.shape[1])
    kv = jnp.dot(local_rows, proj_all, preferred_element_type=jnp.float32).astype(jnp.bfloat16)
    marks = segment[0].astype(jnp.bfloat16)
    marks_row = jnp.pad(marks, (0, 2 * HEAD_DIM - tok_rows))[None, :]
    kvm = jnp.concatenate([kv, marks_row], axis=0)[None]
    kvm_all = pair_gather(kvm, ctx_far, 0)
    keys = kvm_all[:, :tok_rows, :HEAD_DIM].reshape(-1, HEAD_DIM)
    values = kvm_all[:, :tok_rows, HEAD_DIM:].reshape(-1, HEAD_DIM)
    marks_all = kvm_all[:, tok_rows, :tok_rows].reshape(-1)

    mq = marks.astype(jnp.float32)[:, None]
    mk = marks_all.astype(jnp.float32)[None, :]
    grad_q, kv_part = attention_block(queries[0], grad_out[0], keys, values, mq, mk)
    kv_blocks = kv_part.reshape((-1, tok_rows, kv_part.shape[1]))
    kv_grad = pair_scatter(kv_blocks, ctx_far, 2).astype(jnp.bfloat16)

    dims_t = (((0,), (0,)), ((), ()))
    parts = lax.dot_general(local_rows, kv_grad, dims_t, preferred_element_type=jnp.float32)
    parts = parts.astype(jnp.bfloat16)
    parts = parts.reshape((-1, key_proj.shape[0], parts.shape[1]))
    summed = pair_scatter(parts, far_first, 3, canonical)
    key_sum, value_sum = summed[:, :width_kv], summed[:, width_kv:]
    grad_queries = grad_q[None]
    return (grad_queries, key_sum, value_sum)


def solution(mesh):
    placed = (
        P("dp", "context", None),
        P("dp", "context", "head"),
        P("dp", "context", "head"),
        P("dp", "context"),
        P(("dp", "context"), "head"),
        P(("dp", "context"), "head"),
    )
    return jax.shard_map(
        body,
        mesh=mesh,
        in_specs=placed,
        out_specs=(
            P("dp", "context", "head"),
            P(("dp", "context"), "head"),
            P(("dp", "context"), "head"),
        ),
        check_vma=False,
    )
```

```python
import functools

import jax
import jax.numpy as jnp
from jax import lax
from jax.experimental import pallas as pl
from jax.experimental.pallas import tpu as pltpu
from jax.sharding import PartitionSpec as P

HEADS = 32
KV_HEADS = 8
HEAD_DIM = 128


far_below = -1e30


def _bits(n):
    return n.bit_length() - 1


def _exchange(x, axis, size, bit):
    perm = [(i, i ^ (1 << bit)) for i in range(size)]
    return lax.ppermute(x, axis, perm)


def _my_bit(axis, bit):
    return ((lax.axis_index(axis) >> bit) & 1) == 1


def gather_blocks(x, steps, canon):
    cur = x
    dims = []
    for axis, size, bit in steps:
        recv = _exchange(cur, axis, size, bit)
        mine = _my_bit(axis, bit)
        cur = jnp.where(mine, jnp.stack([recv, cur]), jnp.stack([cur, recv]))
        dims.insert(0, (axis, bit))
    order = [dims.index(c) for c in canon]
    cur = jnp.transpose(cur, order + list(range(len(dims), cur.ndim)))
    return cur.reshape((-1,) + x.shape[1:])


def scatter_sum(x, steps, canon, acc=None):
    nb = len(canon)
    acc = acc or x.dtype
    block = x.shape[0] >> nb
    cur = x.reshape((2,) * nb + (block,) + x.shape[1:])
    dims = list(canon)
    for axis, size, bit in steps:
        at = dims.index((axis, bit))
        lo = lax.index_in_dim(cur, 0, at, keepdims=False)
        hi = lax.index_in_dim(cur, 1, at, keepdims=False)
        mine = _my_bit(axis, bit)
        keep = jnp.where(mine, hi, lo)
        send = jnp.where(mine, lo, hi)
        total = keep.astype(acc) + _exchange(send, axis, size, bit).astype(acc)
        cur = total if len(dims) == 1 else total.astype(x.dtype)
        dims.pop(at)
    return cur


def gather_relative(x, steps):
    cur = x
    for axis, size, bit in steps:
        cur = jnp.stack([cur, _exchange(cur, axis, size, bit)])
    return cur


def scatter_relative(x, steps):
    dims = [bit for _, _, bit in steps][::-1]
    cur = x
    for axis, size, bit in steps[::-1]:
        at = dims.index(bit)
        keep = lax.index_in_dim(cur, 0, at, keepdims=False)
        send = lax.index_in_dim(cur, 1, at, keepdims=False)
        total = keep.astype(jnp.float32) + _exchange(send, axis, size, bit).astype(jnp.float32)
        cur = total if len(dims) == 1 else total.astype(x.dtype)
        dims.pop(at)
    return cur


def _gather_kernel(steps, canonical, x_ref, o_ref, held, send_sems, recv_sems, local_sem):
    mesh = pl.DeviceIdType.MESH
    partners = [{axis: lax.bitwise_xor(lax.axis_index(axis), 1 << bit)} for axis, _, bit in steps]
    barrier = pltpu.get_barrier_semaphore()
    for p in partners:
        pl.semaphore_signal(barrier, inc=1, device_id=p, device_id_type=mesh)
    pl.semaphore_wait(barrier, len(partners))
    local = pltpu.make_async_copy(x_ref, held.at[0:1], local_sem)
    local.start()
    sends = []

    def push(src, lo, hi, j):
        base = 1 << j
        copy = pltpu.make_async_remote_copy(
            src_ref=src,
            dst_ref=held.at[base + lo:base + hi],
            send_sem=send_sems.at[len(sends)],
            recv_sem=recv_sems.at[j],
            device_id=partners[j],
            device_id_type=mesh,
        )
        copy.start()
        sends.append(copy)

    for j in range(len(partners)):
        push(x_ref, 0, 1, j)
    for i in range(len(partners)):
        lo, hi = 1 << i, 2 << i
        arrived = pltpu.make_async_remote_copy(
            src_ref=held.at[lo:hi],
            dst_ref=held.at[lo:hi],
            send_sem=send_sems.at[0],
            recv_sem=recv_sems.at[i],
            device_id=partners[i],
            device_id_type=mesh,
        )
        arrived.wait_recv()
        for j in range(i + 1, len(partners)):
            push(held.at[lo:hi], lo, hi, j)
    for copy in sends:
        copy.wait_send()
    local.wait()
    if canonical is None:
        out = pltpu.make_async_copy(held, o_ref, local_sem)
        out.start()
        out.wait()
        return
    weights = []
    me = 0
    for axis, size, bit in steps:
        idx = lax.axis_index(axis)
        mine = (idx // (1 << bit)) % 2
        weights.append(canonical[(axis, bit)] * (1 - 2 * mine))
    for axis, stride in canonical["origin"]:
        me = me + lax.axis_index(axis) * stride
    for r in range(1 << len(steps)):
        at = me
        for k in range(len(steps)):
            if (r >> k) & 1:
                at = at + weights[k]
        pltpu.make_async_copy(held.at[r:r + 1], o_ref.at[pl.ds(at, 1)], local_sem).start()
    pltpu.make_async_copy(held, o_ref, local_sem).wait()


def pair_gather(x, steps, collective_id, canonical=None):
    n = 1 << len(steps)
    shape = (n,) + x.shape[1:]
    return pl.pallas_call(
        functools.partial(_gather_kernel, steps, canonical),
        out_shape=jax.ShapeDtypeStruct(shape, x.dtype),
        in_specs=[pl.BlockSpec(memory_space=pltpu.VMEM)],
        out_specs=pl.BlockSpec(memory_space=pltpu.VMEM),
        scratch_shapes=[
            pltpu.VMEM(shape, x.dtype),
            pltpu.SemaphoreType.DMA((len(steps) * (len(steps) + 1) // 2,)),
            pltpu.SemaphoreType.DMA((len(steps),)),
            pltpu.SemaphoreType.DMA,
        ],
        compiler_params=pltpu.CompilerParams(collective_id=collective_id, has_side_effects=True),
    )(x)


def _scatter_kernel(steps, canonical, x_in, o_ref, acc, rbuf, sbuf, staged, rel, send_sems, recv_sems, local_sem):
    mesh = pl.DeviceIdType.MESH
    partners = [{axis: lax.bitwise_xor(lax.axis_index(axis), 1 << bit)} for axis, _, bit in steps]
    x_ref = x_in
    if canonical is not None:
        weights = []
        me = 0
        for axis, size, bit in steps:
            mine = (lax.axis_index(axis) // (1 << bit)) % 2
            weights.append(canonical[(axis, bit)] * (1 - 2 * mine))
        for axis, stride in canonical["origin"]:
            me = me + lax.axis_index(axis) * stride
        for r in range(1 << len(steps)):
            at = me
            for k in range(len(steps)):
                if (r >> k) & 1:
                    at = at + weights[k]
            pltpu.make_async_copy(x_in.at[pl.ds(at, 1)], rel.at[r:r + 1], local_sem).start()
        pltpu.make_async_copy(x_in, rel, local_sem).wait()
        x_ref = rel
    barrier = pltpu.get_barrier_semaphore()
    for p in partners:
        pl.semaphore_signal(barrier, inc=1, device_id=p, device_id_type=mesh)
    pl.semaphore_wait(barrier, len(partners))
    for k in reversed(range(len(steps))):
        half = 1 << k
        off = half - 1
        if k == len(steps) - 1:
            src = x_ref.at[half:2 * half]
        else:
            sbuf[off:off + half] = acc[half:2 * half].astype(sbuf.dtype)
            stage = pltpu.make_async_copy(sbuf.at[off:off + half], staged.at[off:off + half], local_sem)
            stage.start()
            stage.wait()
            src = staged.at[off:off + half]
        copy = pltpu.make_async_remote_copy(
            src_ref=src,
            dst_ref=rbuf.at[off:off + half],
            send_sem=send_sems.at[k],
            recv_sem=recv_sems.at[k],
            device_id=partners[k],
            device_id_type=mesh,
        )
        copy.start()
        copy.wait()
        got = rbuf[off:off + half].astype(jnp.float32)
        if k == len(steps) - 1:
            acc[0:half] = x_ref[0:half].astype(jnp.float32) + got
        else:
            acc[0:half] = acc[0:half] + got
    o_ref[...] = acc[0]


def pair_scatter(x, steps, collective_id, canonical=None):
    n = x.shape[0]
    block = x.shape[1:]
    return pl.pallas_call(
        functools.partial(_scatter_kernel, steps, canonical),
        out_shape=jax.ShapeDtypeStruct(block, jnp.float32),
        in_specs=[pl.BlockSpec(memory_space=pltpu.VMEM)],
        out_specs=pl.BlockSpec(memory_space=pltpu.VMEM),
        scratch_shapes=[
            pltpu.VMEM((n // 2,) + block, jnp.float32),
            pltpu.VMEM((n - 1,) + block, x.dtype),
            pltpu.VMEM((n - 1,) + block, x.dtype),
            pltpu.VMEM((n - 1,) + block, x.dtype),
            pltpu.VMEM((n if canonical else 1,) + block, x.dtype),
            pltpu.SemaphoreType.DMA((len(steps),)),
            pltpu.SemaphoreType.DMA((len(steps),)),
            pltpu.SemaphoreType.DMA,
        ],
        compiler_params=pltpu.CompilerParams(collective_id=collective_id, has_side_effects=True),
    )(x)


def _attention_kernel(q_ref, do_ref, kvm_ref, mq_ref, mk_ref, gq_ref, dkv_ref, dk_acc, dv_acc, k_scr, v_scr):
    scale = HEAD_DIM ** (-0.5)
    rows = q_ref.shape[0]
    for j in range(kvm_ref.shape[0]):
        k_scr[j * rows:(j + 1) * rows, :] = kvm_ref[j, 0:rows, 0:HEAD_DIM]
        v_scr[j * rows:(j + 1) * rows, :] = kvm_ref[j, 0:rows, HEAD_DIM:2 * HEAD_DIM]
    keys = k_scr[...]
    values = v_scr[...]
    same = mq_ref[...] == mk_ref[...]
    dk_acc[...] = jnp.zeros_like(dk_acc)
    dv_acc[...] = jnp.zeros_like(dv_acc)
    nt = (((1,), (1,)), ((), ()))
    for h in range(q_ref.shape[1] // HEAD_DIM):
        cols = slice(h * HEAD_DIM, (h + 1) * HEAD_DIM)
        qh = q_ref[:, cols]
        doh = do_ref[:, cols]
        raw = lax.dot_general(qh, keys, nt, preferred_element_type=jnp.float32) * scale
        raw = jnp.where(same, raw, far_below)
        top = jnp.max(raw, axis=1, keepdims=True)
        total = jnp.sum(jnp.exp(raw - top), axis=1, keepdims=True)
        probs = jnp.exp(raw - (top + jnp.log(total)))
        probs_b = probs.astype(jnp.bfloat16)
        out = jnp.dot(probs_b, values, preferred_element_type=jnp.float32).astype(jnp.bfloat16)
        delta = jnp.sum(doh.astype(jnp.float32) * out.astype(jnp.float32), axis=1, keepdims=True)
        dv_acc[...] += jnp.dot(probs.T.astype(jnp.bfloat16), doh, preferred_element_type=jnp.float32)
        prob_grad = lax.dot_general(doh, values, nt, preferred_element_type=jnp.float32)
        dscores = probs * (prob_grad - delta)
        gq_ref[:, cols] = (
            jnp.dot(dscores.astype(jnp.bfloat16), keys, preferred_element_type=jnp.float32) * scale
        ).astype(gq_ref.dtype)
        dk_acc[...] += jnp.dot(
            dscores.T.astype(jnp.bfloat16), qh, preferred_element_type=jnp.float32
        ) * scale
    dkv_ref[:, :HEAD_DIM] = dk_acc[...].astype(dkv_ref.dtype)
    dkv_ref[:, HEAD_DIM:] = dv_acc[...].astype(dkv_ref.dtype)


def attention_block(q, do, kvm, mq, mk):
    rows, width = q.shape
    n_keys = kvm.shape[0] * rows
    heads = width // HEAD_DIM
    flops = 2 * rows * n_keys * HEAD_DIM * heads * 6
    vmem = pltpu.VMEM
    return pl.pallas_call(
        _attention_kernel,
        out_shape=(
            jax.ShapeDtypeStruct((rows, width), jnp.bfloat16),
            jax.ShapeDtypeStruct((n_keys, 2 * HEAD_DIM), jnp.bfloat16),
        ),
        in_specs=[pl.BlockSpec(memory_space=vmem)] * 5,
        out_specs=(pl.BlockSpec(memory_space=vmem), pl.BlockSpec(memory_space=vmem)),
        scratch_shapes=[
            pltpu.VMEM((n_keys, HEAD_DIM), jnp.float32),
            pltpu.VMEM((n_keys, HEAD_DIM), jnp.float32),
            pltpu.VMEM((n_keys, HEAD_DIM), kvm.dtype),
            pltpu.VMEM((n_keys, HEAD_DIM), kvm.dtype),
        ],
        cost_estimate=pl.CostEstimate(
            flops=flops,
            transcendentals=2 * rows * n_keys * heads,
            bytes_accessed=4 * rows * width * 2 + 4 * n_keys * HEAD_DIM * 2,
        ),
    )(q, do, kvm, mq, mk)


def body(hidden, queries, grad_out, segment, key_proj, value_proj):
    tok_rows = hidden.shape[1]
    n_dp = lax.axis_size("dp")
    n_ctx = lax.axis_size("context")
    group = HEADS // KV_HEADS
    scale = HEAD_DIM ** (-0.5)
    width_kv = key_proj.shape[1]
    local_rows = hidden[0]

    ctx_canon = [("context", b) for b in reversed(range(_bits(n_ctx)))]
    dp_canon = [("dp", b) for b in reversed(range(_bits(n_dp)))]
    both_canon = dp_canon + ctx_canon

    def step(axis, bit):
        return (axis, n_dp if axis == "dp" else n_ctx, bit)

    ctx_far = [step("context", b) for b in reversed(range(_bits(n_ctx)))]
    dp_far = [step("dp", b) for b in reversed(range(_bits(n_dp)))]
    def interleave(first, second):
        out = []
        for k in range(max(len(first), len(second))):
            out += first[k:k + 1] + second[k:k + 1]
        return out

    order_a = ctx_far[:1] + interleave(ctx_far[1:-1], dp_far) + ctx_far[-1:]
    order_b = ctx_far[:1] + interleave(dp_far, ctx_far[1:-1]) + ctx_far[-1:]

    far_first = ctx_far[:1] + interleave(ctx_far[1:-1], dp_far) + ctx_far[-1:]
    proj = jnp.concatenate([key_proj, value_proj], axis=1)
    canonical = {("dp", b): n_ctx << b for b in range(_bits(n_dp))}
    canonical.update({("context", b): 1 << b for b in range(_bits(n_ctx))})
    canonical["origin"] = (("dp", n_ctx), ("context", 1))
    proj_all = pair_gather(proj[None], far_first, 1, canonical).reshape(-1, proj.shape[1])
    kv = jnp.dot(local_rows, proj_all, preferred_element_type=jnp.float32).astype(jnp.bfloat16)
    marks = segment[0].astype(jnp.bfloat16)
    marks_row = jnp.pad(marks, (0, 2 * HEAD_DIM - tok_rows))[None, :]
    kvm = jnp.concatenate([kv, marks_row], axis=0)[None]
    kvm_all = pair_gather(kvm, ctx_far, 0)
    marks_all = kvm_all[:, tok_rows, :tok_rows].reshape(-1)

    mq = marks.astype(jnp.float32)[:, None]
    mk = marks_all.astype(jnp.float32)[None, :]
    grad_q, kv_part = attention_block(queries[0], grad_out[0], kvm_all, mq, mk)
    kv_blocks = kv_part.reshape((-1, tok_rows, kv_part.shape[1]))
    kv_grad = pair_scatter(kv_blocks, ctx_far, 2).astype(jnp.bfloat16)

    dims_t = (((0,), (0,)), ((), ()))
    parts = lax.dot_general(local_rows, kv_grad, dims_t, preferred_element_type=jnp.float32)
    parts = parts.astype(jnp.bfloat16)
    parts = parts.reshape((-1, key_proj.shape[0], parts.shape[1]))
    summed = pair_scatter(parts, far_first, 3, canonical)
    key_sum, value_sum = summed[:, :width_kv], summed[:, width_kv:]
    grad_queries = grad_q[None]
    return (grad_queries, key_sum, value_sum)


def solution(mesh):
    placed = (
        P("dp", "context", None),
        P("dp", "context", "head"),
        P("dp", "context", "head"),
        P("dp", "context"),
        P(("dp", "context"), "head"),
        P(("dp", "context"), "head"),
    )
    return jax.shard_map(
        body,
        mesh=mesh,
        in_specs=placed,
        out_specs=(
            P("dp", "context", "head"),
            P(("dp", "context"), "head"),
            P(("dp", "context"), "head"),
        ),
        check_vma=False,
    )
```

```python
import functools

import jax
import jax.numpy as jnp
from jax import lax
from jax.experimental import pallas as pl
from jax.experimental.pallas import tpu as pltpu
from jax.sharding import PartitionSpec as P

HEADS = 32
KV_HEADS = 8
HEAD_DIM = 128


far_below = -1e30


def _bits(n):
    return n.bit_length() - 1


def _exchange(x, axis, size, bit):
    perm = [(i, i ^ (1 << bit)) for i in range(size)]
    return lax.ppermute(x, axis, perm)


def _my_bit(axis, bit):
    return ((lax.axis_index(axis) >> bit) & 1) == 1


def gather_blocks(x, steps, canon):
    cur = x
    dims = []
    for axis, size, bit in steps:
        recv = _exchange(cur, axis, size, bit)
        mine = _my_bit(axis, bit)
        cur = jnp.where(mine, jnp.stack([recv, cur]), jnp.stack([cur, recv]))
        dims.insert(0, (axis, bit))
    order = [dims.index(c) for c in canon]
    cur = jnp.transpose(cur, order + list(range(len(dims), cur.ndim)))
    return cur.reshape((-1,) + x.shape[1:])


def scatter_sum(x, steps, canon, acc=None):
    nb = len(canon)
    acc = acc or x.dtype
    block = x.shape[0] >> nb
    cur = x.reshape((2,) * nb + (block,) + x.shape[1:])
    dims = list(canon)
    for axis, size, bit in steps:
        at = dims.index((axis, bit))
        lo = lax.index_in_dim(cur, 0, at, keepdims=False)
        hi = lax.index_in_dim(cur, 1, at, keepdims=False)
        mine = _my_bit(axis, bit)
        keep = jnp.where(mine, hi, lo)
        send = jnp.where(mine, lo, hi)
        total = keep.astype(acc) + _exchange(send, axis, size, bit).astype(acc)
        cur = total if len(dims) == 1 else total.astype(x.dtype)
        dims.pop(at)
    return cur


def gather_relative(x, steps):
    cur = x
    for axis, size, bit in steps:
        cur = jnp.stack([cur, _exchange(cur, axis, size, bit)])
    return cur


def scatter_relative(x, steps):
    dims = [bit for _, _, bit in steps][::-1]
    cur = x
    for axis, size, bit in steps[::-1]:
        at = dims.index(bit)
        keep = lax.index_in_dim(cur, 0, at, keepdims=False)
        send = lax.index_in_dim(cur, 1, at, keepdims=False)
        total = keep.astype(jnp.float32) + _exchange(send, axis, size, bit).astype(jnp.float32)
        cur = total if len(dims) == 1 else total.astype(x.dtype)
        dims.pop(at)
    return cur


def _gather_kernel(steps, canonical, x_ref, o_ref, held, send_sems, recv_sems, local_sem):
    mesh = pl.DeviceIdType.MESH
    partners = [{axis: lax.bitwise_xor(lax.axis_index(axis), 1 << bit)} for axis, _, bit in steps]
    barrier = pltpu.get_barrier_semaphore()
    for p in partners:
        pl.semaphore_signal(barrier, inc=1, device_id=p, device_id_type=mesh)
    pl.semaphore_wait(barrier, len(partners))
    local = pltpu.make_async_copy(x_ref, held.at[0:1], local_sem)
    local.start()
    sends = []

    def push(src, lo, hi, j):
        base = 1 << j
        copy = pltpu.make_async_remote_copy(
            src_ref=src,
            dst_ref=held.at[base + lo:base + hi],
            send_sem=send_sems.at[len(sends)],
            recv_sem=recv_sems.at[j],
            device_id=partners[j],
            device_id_type=mesh,
        )
        copy.start()
        sends.append(copy)

    for j in range(len(partners)):
        push(x_ref, 0, 1, j)
    for i in range(len(partners)):
        lo, hi = 1 << i, 2 << i
        arrived = pltpu.make_async_remote_copy(
            src_ref=held.at[lo:hi],
            dst_ref=held.at[lo:hi],
            send_sem=send_sems.at[0],
            recv_sem=recv_sems.at[i],
            device_id=partners[i],
            device_id_type=mesh,
        )
        arrived.wait_recv()
        for j in range(i + 1, len(partners)):
            push(held.at[lo:hi], lo, hi, j)
    for copy in sends:
        copy.wait_send()
    local.wait()
    if canonical is None:
        out = pltpu.make_async_copy(held, o_ref, local_sem)
        out.start()
        out.wait()
        return
    weights = []
    me = 0
    for axis, size, bit in steps:
        idx = lax.axis_index(axis)
        mine = (idx // (1 << bit)) % 2
        weights.append(canonical[(axis, bit)] * (1 - 2 * mine))
    for axis, stride in canonical["origin"]:
        me = me + lax.axis_index(axis) * stride
    for r in range(1 << len(steps)):
        at = me
        for k in range(len(steps)):
            if (r >> k) & 1:
                at = at + weights[k]
        pltpu.make_async_copy(held.at[r:r + 1], o_ref.at[pl.ds(at, 1)], local_sem).start()
    pltpu.make_async_copy(held, o_ref, local_sem).wait()


def pair_gather(x, steps, collective_id, canonical=None):
    n = 1 << len(steps)
    shape = (n,) + x.shape[1:]
    return pl.pallas_call(
        functools.partial(_gather_kernel, steps, canonical),
        out_shape=jax.ShapeDtypeStruct(shape, x.dtype),
        in_specs=[pl.BlockSpec(memory_space=pltpu.VMEM)],
        out_specs=pl.BlockSpec(memory_space=pltpu.VMEM),
        scratch_shapes=[
            pltpu.VMEM(shape, x.dtype),
            pltpu.SemaphoreType.DMA((len(steps) * (len(steps) + 1) // 2,)),
            pltpu.SemaphoreType.DMA((len(steps),)),
            pltpu.SemaphoreType.DMA,
        ],
        compiler_params=pltpu.CompilerParams(collective_id=collective_id, has_side_effects=True),
    )(x)


def _scatter_kernel(steps, canonical, x_in, o_ref, acc, rbuf, sbuf, staged, rel, send_sems, recv_sems, local_sem):
    mesh = pl.DeviceIdType.MESH
    partners = [{axis: lax.bitwise_xor(lax.axis_index(axis), 1 << bit)} for axis, _, bit in steps]
    x_ref = x_in
    if canonical is not None:
        weights = []
        me = 0
        for axis, size, bit in steps:
            mine = (lax.axis_index(axis) // (1 << bit)) % 2
            weights.append(canonical[(axis, bit)] * (1 - 2 * mine))
        for axis, stride in canonical["origin"]:
            me = me + lax.axis_index(axis) * stride
        for r in range(1 << len(steps)):
            at = me
            for k in range(len(steps)):
                if (r >> k) & 1:
                    at = at + weights[k]
            pltpu.make_async_copy(x_in.at[pl.ds(at, 1)], rel.at[r:r + 1], local_sem).start()
        pltpu.make_async_copy(x_in, rel, local_sem).wait()
        x_ref = rel
    barrier = pltpu.get_barrier_semaphore()
    for p in partners:
        pl.semaphore_signal(barrier, inc=1, device_id=p, device_id_type=mesh)
    pl.semaphore_wait(barrier, len(partners))
    for k in reversed(range(len(steps))):
        half = 1 << k
        off = half - 1
        if k == len(steps) - 1:
            src = x_ref.at[half:2 * half]
        else:
            sbuf[off:off + half] = acc[half:2 * half].astype(sbuf.dtype)
            stage = pltpu.make_async_copy(sbuf.at[off:off + half], staged.at[off:off + half], local_sem)
            stage.start()
            stage.wait()
            src = staged.at[off:off + half]
        copy = pltpu.make_async_remote_copy(
            src_ref=src,
            dst_ref=rbuf.at[off:off + half],
            send_sem=send_sems.at[k],
            recv_sem=recv_sems.at[k],
            device_id=partners[k],
            device_id_type=mesh,
        )
        copy.start()
        copy.wait()
        got = rbuf[off:off + half].astype(jnp.float32)
        if k == len(steps) - 1:
            acc[0:half] = x_ref[0:half].astype(jnp.float32) + got
        else:
            acc[0:half] = acc[0:half] + got
    o_ref[...] = acc[0]


def pair_scatter(x, steps, collective_id, canonical=None):
    n = x.shape[0]
    block = x.shape[1:]
    return pl.pallas_call(
        functools.partial(_scatter_kernel, steps, canonical),
        out_shape=jax.ShapeDtypeStruct(block, jnp.float32),
        in_specs=[pl.BlockSpec(memory_space=pltpu.VMEM)],
        out_specs=pl.BlockSpec(memory_space=pltpu.VMEM),
        scratch_shapes=[
            pltpu.VMEM((n // 2,) + block, jnp.float32),
            pltpu.VMEM((n - 1,) + block, x.dtype),
            pltpu.VMEM((n - 1,) + block, x.dtype),
            pltpu.VMEM((n - 1,) + block, x.dtype),
            pltpu.VMEM((n if canonical else 1,) + block, x.dtype),
            pltpu.SemaphoreType.DMA((len(steps),)),
            pltpu.SemaphoreType.DMA((len(steps),)),
            pltpu.SemaphoreType.DMA,
        ],
        compiler_params=pltpu.CompilerParams(collective_id=collective_id, has_side_effects=True),
    )(x)


def _attention_kernel(q_ref, do_ref, kvm_ref, mq_ref, mk_ref, gq_ref, dkv_ref, dk_acc, dv_acc, k_scr, v_scr):
    scale = HEAD_DIM ** (-0.5)
    rows = q_ref.shape[0]
    for j in range(kvm_ref.shape[0]):
        k_scr[j * rows:(j + 1) * rows, :] = kvm_ref[j, 0:rows, 0:HEAD_DIM]
        v_scr[j * rows:(j + 1) * rows, :] = kvm_ref[j, 0:rows, HEAD_DIM:2 * HEAD_DIM]
    keys = k_scr[...]
    values = v_scr[...]
    same = mq_ref[...] == mk_ref[...]
    dk_acc[...] = jnp.zeros_like(dk_acc)
    dv_acc[...] = jnp.zeros_like(dv_acc)
    nt = (((1,), (1,)), ((), ()))
    for h in range(q_ref.shape[1] // HEAD_DIM):
        cols = slice(h * HEAD_DIM, (h + 1) * HEAD_DIM)
        qh = q_ref[:, cols]
        doh = do_ref[:, cols]
        raw = lax.dot_general(qh, keys, nt, preferred_element_type=jnp.float32) * scale
        raw = jnp.where(same, raw, far_below)
        top = jnp.max(raw, axis=1, keepdims=True)
        weights = jnp.exp(raw - top)
        total = jnp.sum(weights, axis=1, keepdims=True)
        probs = weights / total
        probs_b = probs.astype(jnp.bfloat16)
        out = jnp.dot(probs_b, values, preferred_element_type=jnp.float32).astype(jnp.bfloat16)
        delta = jnp.sum(doh.astype(jnp.float32) * out.astype(jnp.float32), axis=1, keepdims=True)
        dv_acc[...] += jnp.dot(probs.T.astype(jnp.bfloat16), doh, preferred_element_type=jnp.float32)
        prob_grad = lax.dot_general(doh, values, nt, preferred_element_type=jnp.float32)
        dscores = probs * (prob_grad - delta)
        gq_ref[:, cols] = (
            jnp.dot(dscores.astype(jnp.bfloat16), keys, preferred_element_type=jnp.float32) * scale
        ).astype(gq_ref.dtype)
        dk_acc[...] += jnp.dot(
            dscores.T.astype(jnp.bfloat16), qh, preferred_element_type=jnp.float32
        ) * scale
    dkv_ref[:, :HEAD_DIM] = dk_acc[...].astype(dkv_ref.dtype)
    dkv_ref[:, HEAD_DIM:] = dv_acc[...].astype(dkv_ref.dtype)


def attention_block(q, do, kvm, mq, mk):
    rows, width = q.shape
    n_keys = kvm.shape[0] * rows
    heads = width // HEAD_DIM
    flops = 2 * rows * n_keys * HEAD_DIM * heads * 6
    vmem = pltpu.VMEM
    return pl.pallas_call(
        _attention_kernel,
        out_shape=(
            jax.ShapeDtypeStruct((rows, width), jnp.bfloat16),
            jax.ShapeDtypeStruct((n_keys, 2 * HEAD_DIM), jnp.bfloat16),
        ),
        in_specs=[pl.BlockSpec(memory_space=vmem)] * 5,
        out_specs=(pl.BlockSpec(memory_space=vmem), pl.BlockSpec(memory_space=vmem)),
        scratch_shapes=[
            pltpu.VMEM((n_keys, HEAD_DIM), jnp.float32),
            pltpu.VMEM((n_keys, HEAD_DIM), jnp.float32),
            pltpu.VMEM((n_keys, HEAD_DIM), kvm.dtype),
            pltpu.VMEM((n_keys, HEAD_DIM), kvm.dtype),
        ],
        cost_estimate=pl.CostEstimate(
            flops=flops,
            transcendentals=2 * rows * n_keys * heads,
            bytes_accessed=4 * rows * width * 2 + 4 * n_keys * HEAD_DIM * 2,
        ),
    )(q, do, kvm, mq, mk)


def body(hidden, queries, grad_out, segment, key_proj, value_proj):
    tok_rows = hidden.shape[1]
    n_dp = lax.axis_size("dp")
    n_ctx = lax.axis_size("context")
    group = HEADS // KV_HEADS
    scale = HEAD_DIM ** (-0.5)
    width_kv = key_proj.shape[1]
    local_rows = hidden[0]

    ctx_canon = [("context", b) for b in reversed(range(_bits(n_ctx)))]
    dp_canon = [("dp", b) for b in reversed(range(_bits(n_dp)))]
    both_canon = dp_canon + ctx_canon

    def step(axis, bit):
        return (axis, n_dp if axis == "dp" else n_ctx, bit)

    ctx_far = [step("context", b) for b in reversed(range(_bits(n_ctx)))]
    dp_far = [step("dp", b) for b in reversed(range(_bits(n_dp)))]
    def interleave(first, second):
        out = []
        for k in range(max(len(first), len(second))):
            out += first[k:k + 1] + second[k:k + 1]
        return out

    order_a = ctx_far[:1] + interleave(ctx_far[1:-1], dp_far) + ctx_far[-1:]
    order_b = ctx_far[:1] + interleave(dp_far, ctx_far[1:-1]) + ctx_far[-1:]

    far_first = ctx_far[:1] + interleave(ctx_far[1:-1], dp_far) + ctx_far[-1:]
    proj = jnp.concatenate([key_proj, value_proj], axis=1)
    canonical = {("dp", b): n_ctx << b for b in range(_bits(n_dp))}
    canonical.update({("context", b): 1 << b for b in range(_bits(n_ctx))})
    canonical["origin"] = (("dp", n_ctx), ("context", 1))
    proj_all = pair_gather(proj[None], far_first, 1, canonical).reshape(-1, proj.shape[1])
    kv = jnp.dot(local_rows, proj_all, preferred_element_type=jnp.float32).astype(jnp.bfloat16)
    marks = segment[0].astype(jnp.bfloat16)
    marks_row = jnp.pad(marks, (0, 2 * HEAD_DIM - tok_rows))[None, :]
    kvm = jnp.concatenate([kv, marks_row], axis=0)[None]
    kvm_all = pair_gather(kvm, ctx_far, 0)
    marks_all = kvm_all[:, tok_rows, :tok_rows].reshape(-1)

    mq = marks.astype(jnp.float32)[:, None]
    mk = marks_all.astype(jnp.float32)[None, :]
    grad_q, kv_part = attention_block(queries[0], grad_out[0], kvm_all, mq, mk)
    kv_blocks = kv_part.reshape((-1, tok_rows, kv_part.shape[1]))
    kv_grad = pair_scatter(kv_blocks, ctx_far, 2).astype(jnp.bfloat16)

    dims_t = (((0,), (0,)), ((), ()))
    parts = lax.dot_general(local_rows, kv_grad, dims_t, preferred_element_type=jnp.float32)
    parts = parts.astype(jnp.bfloat16)
    parts = parts.reshape((-1, key_proj.shape[0], parts.shape[1]))
    summed = pair_scatter(parts, far_first, 3, canonical)
    key_sum, value_sum = summed[:, :width_kv], summed[:, width_kv:]
    grad_queries = grad_q[None]
    return (grad_queries, key_sum, value_sum)


def solution(mesh):
    placed = (
        P("dp", "context", None),
        P("dp", "context", "head"),
        P("dp", "context", "head"),
        P("dp", "context"),
        P(("dp", "context"), "head"),
        P(("dp", "context"), "head"),
    )
    return jax.shard_map(
        body,
        mesh=mesh,
        in_specs=placed,
        out_specs=(
            P("dp", "context", "head"),
            P(("dp", "context"), "head"),
            P(("dp", "context"), "head"),
        ),
        check_vma=False,
    )
```

```python
import functools

import jax
import jax.numpy as jnp
from jax import lax
from jax.experimental import pallas as pl
from jax.experimental.pallas import tpu as pltpu
from jax.sharding import PartitionSpec as P

HEADS = 32
KV_HEADS = 8
HEAD_DIM = 128


far_below = -1e30


def _bits(n):
    return n.bit_length() - 1


def _exchange(x, axis, size, bit):
    perm = [(i, i ^ (1 << bit)) for i in range(size)]
    return lax.ppermute(x, axis, perm)


def _my_bit(axis, bit):
    return ((lax.axis_index(axis) >> bit) & 1) == 1


def gather_blocks(x, steps, canon):
    cur = x
    dims = []
    for axis, size, bit in steps:
        recv = _exchange(cur, axis, size, bit)
        mine = _my_bit(axis, bit)
        cur = jnp.where(mine, jnp.stack([recv, cur]), jnp.stack([cur, recv]))
        dims.insert(0, (axis, bit))
    order = [dims.index(c) for c in canon]
    cur = jnp.transpose(cur, order + list(range(len(dims), cur.ndim)))
    return cur.reshape((-1,) + x.shape[1:])


def scatter_sum(x, steps, canon, acc=None):
    nb = len(canon)
    acc = acc or x.dtype
    block = x.shape[0] >> nb
    cur = x.reshape((2,) * nb + (block,) + x.shape[1:])
    dims = list(canon)
    for axis, size, bit in steps:
        at = dims.index((axis, bit))
        lo = lax.index_in_dim(cur, 0, at, keepdims=False)
        hi = lax.index_in_dim(cur, 1, at, keepdims=False)
        mine = _my_bit(axis, bit)
        keep = jnp.where(mine, hi, lo)
        send = jnp.where(mine, lo, hi)
        total = keep.astype(acc) + _exchange(send, axis, size, bit).astype(acc)
        cur = total if len(dims) == 1 else total.astype(x.dtype)
        dims.pop(at)
    return cur


def gather_relative(x, steps):
    cur = x
    for axis, size, bit in steps:
        cur = jnp.stack([cur, _exchange(cur, axis, size, bit)])
    return cur


def scatter_relative(x, steps):
    dims = [bit for _, _, bit in steps][::-1]
    cur = x
    for axis, size, bit in steps[::-1]:
        at = dims.index(bit)
        keep = lax.index_in_dim(cur, 0, at, keepdims=False)
        send = lax.index_in_dim(cur, 1, at, keepdims=False)
        total = keep.astype(jnp.float32) + _exchange(send, axis, size, bit).astype(jnp.float32)
        cur = total if len(dims) == 1 else total.astype(x.dtype)
        dims.pop(at)
    return cur


def _gather_kernel(steps, canonical, x_ref, o_ref, held, send_sems, recv_sems, local_sem):
    mesh = pl.DeviceIdType.MESH
    partners = [{axis: lax.bitwise_xor(lax.axis_index(axis), 1 << bit)} for axis, _, bit in steps]
    barrier = pltpu.get_barrier_semaphore()
    for p in partners:
        pl.semaphore_signal(barrier, inc=1, device_id=p, device_id_type=mesh)
    pl.semaphore_wait(barrier, len(partners))
    local = pltpu.make_async_copy(x_ref, held.at[0:1], local_sem)
    local.start()
    sends = []

    def push(src, lo, hi, j):
        base = 1 << j
        copy = pltpu.make_async_remote_copy(
            src_ref=src,
            dst_ref=held.at[base + lo:base + hi],
            send_sem=send_sems.at[len(sends)],
            recv_sem=recv_sems.at[j],
            device_id=partners[j],
            device_id_type=mesh,
        )
        copy.start()
        sends.append(copy)

    for j in range(len(partners)):
        push(x_ref, 0, 1, j)
    for i in range(len(partners)):
        lo, hi = 1 << i, 2 << i
        arrived = pltpu.make_async_remote_copy(
            src_ref=held.at[lo:hi],
            dst_ref=held.at[lo:hi],
            send_sem=send_sems.at[0],
            recv_sem=recv_sems.at[i],
            device_id=partners[i],
            device_id_type=mesh,
        )
        arrived.wait_recv()
        for j in range(i + 1, len(partners)):
            push(held.at[lo:hi], lo, hi, j)
    for copy in sends:
        copy.wait_send()
    local.wait()
    if canonical is None:
        out = pltpu.make_async_copy(held, o_ref, local_sem)
        out.start()
        out.wait()
        return
    weights = []
    me = 0
    for axis, size, bit in steps:
        idx = lax.axis_index(axis)
        mine = (idx // (1 << bit)) % 2
        weights.append(canonical[(axis, bit)] * (1 - 2 * mine))
    for axis, stride in canonical["origin"]:
        me = me + lax.axis_index(axis) * stride
    for r in range(1 << len(steps)):
        at = me
        for k in range(len(steps)):
            if (r >> k) & 1:
                at = at + weights[k]
        pltpu.make_async_copy(held.at[r:r + 1], o_ref.at[pl.ds(at, 1)], local_sem).start()
    pltpu.make_async_copy(held, o_ref, local_sem).wait()


def pair_gather(x, steps, collective_id, canonical=None):
    n = 1 << len(steps)
    shape = (n,) + x.shape[1:]
    return pl.pallas_call(
        functools.partial(_gather_kernel, steps, canonical),
        out_shape=jax.ShapeDtypeStruct(shape, x.dtype),
        in_specs=[pl.BlockSpec(memory_space=pltpu.VMEM)],
        out_specs=pl.BlockSpec(memory_space=pltpu.VMEM),
        scratch_shapes=[
            pltpu.VMEM(shape, x.dtype),
            pltpu.SemaphoreType.DMA((len(steps) * (len(steps) + 1) // 2,)),
            pltpu.SemaphoreType.DMA((len(steps),)),
            pltpu.SemaphoreType.DMA,
        ],
        compiler_params=pltpu.CompilerParams(collective_id=collective_id, has_side_effects=True),
    )(x)


def _scatter_kernel(steps, canonical, x_in, o_ref, acc, rbuf, sbuf, staged, rel, send_sems, recv_sems, local_sem):
    mesh = pl.DeviceIdType.MESH
    partners = [{axis: lax.bitwise_xor(lax.axis_index(axis), 1 << bit)} for axis, _, bit in steps]
    barrier = pltpu.get_barrier_semaphore()
    for p in partners:
        pl.semaphore_signal(barrier, inc=1, device_id=p, device_id_type=mesh)
    x_ref = x_in
    if canonical is not None:
        weights = []
        me = 0
        for axis, size, bit in steps:
            mine = (lax.axis_index(axis) // (1 << bit)) % 2
            weights.append(canonical[(axis, bit)] * (1 - 2 * mine))
        for axis, stride in canonical["origin"]:
            me = me + lax.axis_index(axis) * stride
        for r in range(1 << len(steps)):
            at = me
            for k in range(len(steps)):
                if (r >> k) & 1:
                    at = at + weights[k]
            pltpu.make_async_copy(x_in.at[pl.ds(at, 1)], rel.at[r:r + 1], local_sem).start()
        pltpu.make_async_copy(x_in, rel, local_sem).wait()
        x_ref = rel
    pl.semaphore_wait(barrier, len(partners))
    for k in reversed(range(len(steps))):
        half = 1 << k
        off = half - 1
        if k == len(steps) - 1:
            src = x_ref.at[half:2 * half]
        else:
            sbuf[off:off + half] = acc[half:2 * half].astype(sbuf.dtype)
            stage = pltpu.make_async_copy(sbuf.at[off:off + half], staged.at[off:off + half], local_sem)
            stage.start()
            stage.wait()
            src = staged.at[off:off + half]
        copy = pltpu.make_async_remote_copy(
            src_ref=src,
            dst_ref=rbuf.at[off:off + half],
            send_sem=send_sems.at[k],
            recv_sem=recv_sems.at[k],
            device_id=partners[k],
            device_id_type=mesh,
        )
        copy.start()
        copy.wait()
        got = rbuf[off:off + half].astype(jnp.float32)
        if k == len(steps) - 1:
            acc[0:half] = x_ref[0:half].astype(jnp.float32) + got
        else:
            acc[0:half] = acc[0:half] + got
    o_ref[...] = acc[0]


def pair_scatter(x, steps, collective_id, canonical=None):
    n = x.shape[0]
    block = x.shape[1:]
    return pl.pallas_call(
        functools.partial(_scatter_kernel, steps, canonical),
        out_shape=jax.ShapeDtypeStruct(block, jnp.float32),
        in_specs=[pl.BlockSpec(memory_space=pltpu.VMEM)],
        out_specs=pl.BlockSpec(memory_space=pltpu.VMEM),
        scratch_shapes=[
            pltpu.VMEM((n // 2,) + block, jnp.float32),
            pltpu.VMEM((n - 1,) + block, x.dtype),
            pltpu.VMEM((n - 1,) + block, x.dtype),
            pltpu.VMEM((n - 1,) + block, x.dtype),
            pltpu.VMEM((n if canonical else 1,) + block, x.dtype),
            pltpu.SemaphoreType.DMA((len(steps),)),
            pltpu.SemaphoreType.DMA((len(steps),)),
            pltpu.SemaphoreType.DMA,
        ],
        compiler_params=pltpu.CompilerParams(collective_id=collective_id, has_side_effects=True),
    )(x)


def _attention_kernel(q_ref, do_ref, kvm_ref, mq_ref, mk_ref, gq_ref, dkv_ref, dk_acc, dv_acc, k_scr, v_scr):
    scale = HEAD_DIM ** (-0.5)
    rows = q_ref.shape[0]
    for j in range(kvm_ref.shape[0]):
        k_scr[j * rows:(j + 1) * rows, :] = kvm_ref[j, 0:rows, 0:HEAD_DIM]
        v_scr[j * rows:(j + 1) * rows, :] = kvm_ref[j, 0:rows, HEAD_DIM:2 * HEAD_DIM]
    keys = k_scr[...]
    values = v_scr[...]
    same = mq_ref[...] == mk_ref[...]
    dk_acc[...] = jnp.zeros_like(dk_acc)
    dv_acc[...] = jnp.zeros_like(dv_acc)
    nt = (((1,), (1,)), ((), ()))
    for h in range(q_ref.shape[1] // HEAD_DIM):
        cols = slice(h * HEAD_DIM, (h + 1) * HEAD_DIM)
        qh = q_ref[:, cols]
        doh = do_ref[:, cols]
        raw = lax.dot_general(qh, keys, nt, preferred_element_type=jnp.float32) * scale
        raw = jnp.where(same, raw, far_below)
        top = jnp.max(raw, axis=1, keepdims=True)
        total = jnp.sum(jnp.exp(raw - top), axis=1, keepdims=True)
        probs = jnp.exp(raw - (top + jnp.log(total)))
        probs_b = probs.astype(jnp.bfloat16)
        out = jnp.dot(probs_b, values, preferred_element_type=jnp.float32).astype(jnp.bfloat16)
        delta = jnp.sum(doh.astype(jnp.float32) * out.astype(jnp.float32), axis=1, keepdims=True)
        dv_acc[...] += jnp.dot(probs.T.astype(jnp.bfloat16), doh, preferred_element_type=jnp.float32)
        prob_grad = lax.dot_general(doh, values, nt, preferred_element_type=jnp.float32)
        dscores = probs * (prob_grad - delta)
        gq_ref[:, cols] = (
            jnp.dot(dscores.astype(jnp.bfloat16), keys, preferred_element_type=jnp.float32) * scale
        ).astype(gq_ref.dtype)
        dk_acc[...] += jnp.dot(
            dscores.T.astype(jnp.bfloat16), qh, preferred_element_type=jnp.float32
        ) * scale
    dkv_ref[:, :HEAD_DIM] = dk_acc[...].astype(dkv_ref.dtype)
    dkv_ref[:, HEAD_DIM:] = dv_acc[...].astype(dkv_ref.dtype)


def attention_block(q, do, kvm, mq, mk):
    rows, width = q.shape
    n_keys = kvm.shape[0] * rows
    heads = width // HEAD_DIM
    flops = 2 * rows * n_keys * HEAD_DIM * heads * 6
    vmem = pltpu.VMEM
    return pl.pallas_call(
        _attention_kernel,
        out_shape=(
            jax.ShapeDtypeStruct((rows, width), jnp.bfloat16),
            jax.ShapeDtypeStruct((n_keys, 2 * HEAD_DIM), jnp.bfloat16),
        ),
        in_specs=[pl.BlockSpec(memory_space=vmem)] * 5,
        out_specs=(pl.BlockSpec(memory_space=vmem), pl.BlockSpec(memory_space=vmem)),
        scratch_shapes=[
            pltpu.VMEM((n_keys, HEAD_DIM), jnp.float32),
            pltpu.VMEM((n_keys, HEAD_DIM), jnp.float32),
            pltpu.VMEM((n_keys, HEAD_DIM), kvm.dtype),
            pltpu.VMEM((n_keys, HEAD_DIM), kvm.dtype),
        ],
        cost_estimate=pl.CostEstimate(
            flops=flops,
            transcendentals=2 * rows * n_keys * heads,
            bytes_accessed=4 * rows * width * 2 + 4 * n_keys * HEAD_DIM * 2,
        ),
    )(q, do, kvm, mq, mk)


def body(hidden, queries, grad_out, segment, key_proj, value_proj):
    tok_rows = hidden.shape[1]
    n_dp = lax.axis_size("dp")
    n_ctx = lax.axis_size("context")
    group = HEADS // KV_HEADS
    scale = HEAD_DIM ** (-0.5)
    width_kv = key_proj.shape[1]
    local_rows = hidden[0]

    ctx_canon = [("context", b) for b in reversed(range(_bits(n_ctx)))]
    dp_canon = [("dp", b) for b in reversed(range(_bits(n_dp)))]
    both_canon = dp_canon + ctx_canon

    def step(axis, bit):
        return (axis, n_dp if axis == "dp" else n_ctx, bit)

    ctx_far = [step("context", b) for b in reversed(range(_bits(n_ctx)))]
    dp_far = [step("dp", b) for b in reversed(range(_bits(n_dp)))]
    def interleave(first, second):
        out = []
        for k in range(max(len(first), len(second))):
            out += first[k:k + 1] + second[k:k + 1]
        return out

    order_a = ctx_far[:1] + interleave(ctx_far[1:-1], dp_far) + ctx_far[-1:]
    order_b = ctx_far[:1] + interleave(dp_far, ctx_far[1:-1]) + ctx_far[-1:]

    far_first = ctx_far[:1] + interleave(ctx_far[1:-1], dp_far) + ctx_far[-1:]
    proj = jnp.concatenate([key_proj, value_proj], axis=1)
    canonical = {("dp", b): n_ctx << b for b in range(_bits(n_dp))}
    canonical.update({("context", b): 1 << b for b in range(_bits(n_ctx))})
    canonical["origin"] = (("dp", n_ctx), ("context", 1))
    proj_all = pair_gather(proj[None], far_first, 1, canonical).reshape(-1, proj.shape[1])
    kv = jnp.dot(local_rows, proj_all, preferred_element_type=jnp.float32).astype(jnp.bfloat16)
    marks = segment[0].astype(jnp.bfloat16)
    marks_row = jnp.pad(marks, (0, 2 * HEAD_DIM - tok_rows))[None, :]
    kvm = jnp.concatenate([kv, marks_row], axis=0)[None]
    kvm_all = pair_gather(kvm, ctx_far, 0)
    marks_all = kvm_all[:, tok_rows, :tok_rows].reshape(-1)

    mq = marks.astype(jnp.float32)[:, None]
    mk = marks_all.astype(jnp.float32)[None, :]
    grad_q, kv_part = attention_block(queries[0], grad_out[0], kvm_all, mq, mk)
    kv_blocks = kv_part.reshape((-1, tok_rows, kv_part.shape[1]))
    kv_grad = pair_scatter(kv_blocks, ctx_far, 2).astype(jnp.bfloat16)

    dims_t = (((0,), (0,)), ((), ()))
    parts = lax.dot_general(local_rows, kv_grad, dims_t, preferred_element_type=jnp.float32)
    parts = parts.astype(jnp.bfloat16)
    parts = parts.reshape((-1, key_proj.shape[0], parts.shape[1]))
    summed = pair_scatter(parts, far_first, 3, canonical)
    key_sum, value_sum = summed[:, :width_kv], summed[:, width_kv:]
    grad_queries = grad_q[None]
    return (grad_queries, key_sum, value_sum)


def solution(mesh):
    placed = (
        P("dp", "context", None),
        P("dp", "context", "head"),
        P("dp", "context", "head"),
        P("dp", "context"),
        P(("dp", "context"), "head"),
        P(("dp", "context"), "head"),
    )
    return jax.shard_map(
        body,
        mesh=mesh,
        in_specs=placed,
        out_specs=(
            P("dp", "context", "head"),
            P(("dp", "context"), "head"),
            P(("dp", "context"), "head"),
        ),
        check_vma=False,
    )
```
